32 devices in a mesh: ctx: 16 (over z, y, x), tp: 2 (over core).
Axes of the slice: x: 2, y: 2, z: 4, core: 2. Of those that a mesh axis runs over, the one named last changes fastest.
Arguments:
- tokens: bfloat16 [4096, 2688], P(('ctx', 'tp')), may hold values from -6 to 6
- result_grad: bfloat16 [4096, 2688], P(('ctx', 'tp')), may hold values from -6 to 6
- query_weight: bfloat16 [2688, 512], P(None, 'tp'), may hold values from -0.125 to 0.125
- key_weight: bfloat16 [2688, 256], P(None, 'tp'), may hold values from -0.125 to 0.125
- value_weight: bfloat16 [2688, 256], P(None, 'tp'), may hold values from -0.125 to 0.125
- output_weight: bfloat16 [512, 2688], P('tp'), may hold values from -0.5 to 0.5
- query_gain: float32 [128], replicated, may hold values from 0.5 to 1.5
- key_gain: float32 [128], replicated, may hold values from 0.5 to 1.5
Outputs:
- layer_output: bfloat16 [4096, 2688], P(('ctx', 'tp'))
- tokens_grad: bfloat16 [4096, 2688], P(('ctx', 'tp'))
The draws below stay inside these ranges and needn't reach their ends.
All inputs are finite; a program needn't handle non-finite values.
Results may differ from the reference program's by a relative error of at most 0.012.
Values may be sent and summed in bfloat16 or wider, within the bound.
A program may use at most 64 MiB of HBM per device.

```python
import jax
import jax.numpy as jnp
from jax import lax

D = 2688
HEAD = 128
WINDOW = 1024
T_DEV = 256
TOKENS = 4096
QHEADS = 4
KVHEADS = 2
N_TP = 2


def shard_levels(stream_key, extent, split, low, top_value):
    gain = 1.0
    for position, blocks in split:
        draws = jax.random.uniform(jax.random.fold_in(jax.random.fold_in(stream_key, 6), position), (blocks,), jnp.float32, low / len(split), top_value / len(split))
        gain = gain * jnp.repeat(jnp.exp(draws), extent[position] // blocks).reshape((-1,) + (1,) * (len(extent) - 1 - position))
    return gain


def noise(stream_key, shape, width, reach, cuts=(), held_as=jnp.bfloat16):
    gain = shard_levels(stream_key, shape, cuts, -0.22, 0.18) if cuts else 1.0
    array = jax.random.normal(stream_key, shape, jnp.float32) * width * gain
    return jnp.minimum(jnp.maximum(array, -reach), reach).astype(held_as)


def setup_inputs(seed: int = 0) -> dict:
    keys = jax.random.split(jax.random.key(seed), 9)
    return {
        "tokens": noise(keys[0], (TOKENS, D), 1.0, 6.0, ((0, 32),)),
        "result_grad": noise(keys[1], (TOKENS, D), 1.0, 6.0, ((0, 32),)),
        "query_weight": noise(keys[2], (D, QHEADS * HEAD), D ** -0.5, 0.125, ((1, 2),)),
        "key_weight": noise(keys[3], (D, KVHEADS * HEAD), D ** -0.5, 0.125, ((1, 2),)),
        "value_weight": noise(keys[4], (D, KVHEADS * HEAD), D ** -0.5, 0.125, ((1, 2),)),
        "output_weight": noise(keys[5], (QHEADS * HEAD, D), HEAD ** -0.5, 0.5, ((0, 2),)),
        "query_gain": jnp.clip(1.0 + 0.1 * jax.random.normal(keys[6], (HEAD,), jnp.float32), 0.5, 1.5),
        "key_gain": jnp.clip(1.0 + 0.1 * jax.random.normal(keys[7], (HEAD,), jnp.float32), 0.5, 1.5),
    }


norm_epsilon = 1e-06
score_scale = 168.0 ** (-0.5)
rope_theta = 10000.0

def rope_tables(positions, head_size):
    half_size = head_size // 2
    exponent = jnp.arange(half_size, dtype=jnp.float32) * (2.0 / head_size)
    frequency = jnp.power(jnp.float32(rope_theta), -exponent)
    angles = positions.astype(jnp.float32)[:, None] * frequency[None, :]
    return (jnp.cos(angles), jnp.sin(angles))

def norm_rope(raw_proj, scale_gain, cosines, sines):
    row_count = raw_proj.shape[0]
    head_size = scale_gain.shape[0]
    split_heads = raw_proj.reshape(row_count, -1, head_size)
    mean_square = lax.optimization_barrier(jnp.mean(split_heads * split_heads, axis=-1, keepdims=True))
    normed = split_heads * lax.rsqrt(mean_square + norm_epsilon) * scale_gain.astype(jnp.float32)
    half_size = head_size // 2
    low_half = normed[..., :half_size]
    high_half = normed[..., half_size:]
    cosine_b = cosines[:, None, :]
    sine_b = sines[:, None, :]
    return jnp.concatenate([low_half * cosine_b - high_half * sine_b, high_half * cosine_b + low_half * sine_b], axis=-1)

def attend(queries, keys_all, values_all, out_grad, query_first, key_first):
    query_count = queries.shape[0]
    key_count = keys_all.shape[0]
    queries_f = queries.astype(jnp.float32)
    keys_f = keys_all.astype(jnp.float32)
    values_f = values_all.astype(jnp.float32)
    out_grad_f = out_grad.astype(jnp.float32)
    scores = jnp.einsum('qkgh,ckh->kgqc', queries_f, keys_f) * score_scale
    query_pos = query_first + jnp.arange(query_count, dtype=jnp.int32)
    key_pos = key_first + jnp.arange(key_count, dtype=jnp.int32)
    distance = query_pos[:, None] - key_pos[None, :]
    allowed = (distance >= 0) & (distance < WINDOW) & (key_pos[None, :] >= 0)
    weights_raw = jnp.where(allowed, jnp.exp(scores), jnp.float32(0.0))
    denominator = lax.optimization_barrier(jnp.sum(weights_raw, axis=-1, keepdims=True))
    weights_soft = weights_raw / denominator
    weights_low = lax.optimization_barrier(weights_soft.astype(jnp.bfloat16))
    weights_low_f = weights_low.astype(jnp.float32)
    attended = lax.optimization_barrier(jnp.einsum('kgqc,ckh->qkgh', weights_low_f, values_f).astype(jnp.bfloat16))
    row_dots = lax.optimization_barrier(jnp.sum(out_grad_f * attended.astype(jnp.float32), axis=-1))
    prob_grad = jnp.einsum('qkgh,ckh->kgqc', out_grad_f, values_f)
    centered = prob_grad - jnp.transpose(row_dots, (1, 2, 0))[..., None]
    score_grad = lax.optimization_barrier((weights_soft * centered * score_scale).astype(jnp.bfloat16))
    score_grad_f = score_grad.astype(jnp.float32)
    query_grad = jnp.einsum('kgqc,ckh->qkgh', score_grad_f, keys_f)
    key_grad = jnp.einsum('kgqc,qkgh->ckh', score_grad_f, queries_f)
    value_grad = jnp.einsum('kgqc,qkgh->ckh', weights_low_f, out_grad_f)
    return (attended, query_grad, key_grad, value_grad)

def group_pass(tokens, result_grad, query_weight, key_weight, value_weight, output_weight, query_gain, key_gain):
    token_count = tokens.shape[0]
    kv_count = key_weight.shape[1] // HEAD
    per_kv = query_weight.shape[1] // key_weight.shape[1]
    positions = jnp.arange(token_count, dtype=jnp.int32)
    cosines, sines = rope_tables(positions, HEAD)
    query_raw = jnp.dot(tokens, query_weight, preferred_element_type=jnp.float32)
    key_raw = jnp.dot(tokens, key_weight, preferred_element_type=jnp.float32)
    value_raw = jnp.dot(tokens, value_weight, preferred_element_type=jnp.float32)
    queries = norm_rope(query_raw, query_gain, cosines, sines).astype(jnp.bfloat16).reshape(token_count, kv_count, per_kv, HEAD)
    keys_all = norm_rope(key_raw, key_gain, cosines, sines).astype(jnp.bfloat16)
    values_all = value_raw.astype(jnp.bfloat16).reshape(token_count, kv_count, HEAD)
    out_grad = jnp.dot(result_grad, output_weight.T, preferred_element_type=jnp.float32).astype(jnp.bfloat16)
    out_grad = out_grad.reshape(token_count, kv_count, per_kv, HEAD)
    padding = jnp.zeros((WINDOW, kv_count, HEAD), jnp.bfloat16)
    keys_pad = jnp.concatenate([padding, keys_all], axis=0)
    values_pad = jnp.concatenate([padding, values_all], axis=0)

    def one_block(running, block_index):
        key_acc, value_acc = running
        first_row = (block_index * T_DEV).astype(jnp.int32)
        query_block = lax.dynamic_slice_in_dim(queries, first_row, T_DEV, 0)
        grad_block = lax.dynamic_slice_in_dim(out_grad, first_row, T_DEV, 0)
        key_block = lax.dynamic_slice_in_dim(keys_pad, first_row, WINDOW + T_DEV, 0)
        value_block = lax.dynamic_slice_in_dim(values_pad, first_row, WINDOW + T_DEV, 0)
        attended, query_grad, key_grad, value_grad = attend(query_block, key_block, value_block, grad_block, first_row, first_row - WINDOW)
        key_acc = lax.dynamic_update_slice_in_dim(key_acc, lax.dynamic_slice_in_dim(key_acc, first_row, WINDOW + T_DEV, 0) + key_grad, first_row, 0)
        value_acc = lax.dynamic_update_slice_in_dim(value_acc, lax.dynamic_slice_in_dim(value_acc, first_row, WINDOW + T_DEV, 0) + value_grad, first_row, 0)
        return ((key_acc, value_acc), (attended, query_grad))
    zeros_acc = jnp.zeros((WINDOW + token_count, kv_count, HEAD), jnp.float32)
    block_ids = jnp.arange(token_count // T_DEV, dtype=jnp.int32)
    (key_acc, value_acc), (attended, query_grad) = lax.scan(one_block, (zeros_acc, zeros_acc), block_ids)
    attended_flat = attended.reshape(token_count, -1)
    query_grad = query_grad.reshape(token_count, -1, HEAD)

    def query_shape(raw_proj):
        return norm_rope(raw_proj, query_gain, cosines, sines)

    def key_shape(raw_proj):
        return norm_rope(raw_proj, key_gain, cosines, sines)
    query_back = jax.vjp(query_shape, query_raw)[1](query_grad)[0].astype(jnp.bfloat16)
    key_back = jax.vjp(key_shape, key_raw)[1](key_acc[WINDOW:])[0].astype(jnp.bfloat16)
    value_back = value_acc[WINDOW:].reshape(token_count, -1).astype(jnp.bfloat16)
    out_part = jnp.dot(attended_flat, output_weight, preferred_element_type=jnp.float32).astype(jnp.bfloat16)
    grad_part = jnp.dot(query_back, query_weight.T, preferred_element_type=jnp.float32)
    grad_part = grad_part + jnp.dot(key_back, key_weight.T, preferred_element_type=jnp.float32)
    grad_part = grad_part + jnp.dot(value_back, value_weight.T, preferred_element_type=jnp.float32)
    return (out_part, grad_part.astype(jnp.bfloat16))

def reference(tokens, result_grad, query_weight, key_weight, value_weight, output_weight, query_gain, key_gain):
    query_cols = query_weight.shape[1] // N_TP
    kv_cols = key_weight.shape[1] // N_TP
    out_sum = tokens.astype(jnp.float32)
    grad_sum = result_grad.astype(jnp.float32)
    for group_index in range(N_TP):
        query_part = query_weight[:, group_index * query_cols:(group_index + 1) * query_cols]
        key_part = key_weight[:, group_index * kv_cols:(group_index + 1) * kv_cols]
        value_part = value_weight[:, group_index * kv_cols:(group_index + 1) * kv_cols]
        output_part = output_weight[group_index * query_cols:(group_index + 1) * query_cols]
        out_part, grad_part = group_pass(tokens, result_grad, query_part, key_part, value_part, output_part, query_gain, key_gain)
        out_sum = out_sum + out_part.astype(jnp.float32)
        grad_sum = grad_sum + grad_part.astype(jnp.float32)
    return (out_sum.astype(jnp.bfloat16), grad_sum.astype(jnp.bfloat16))
```

```python
import functools

import jax
import jax.numpy as jnp
import numpy as np
from jax import lax
from jax.experimental import pallas as pl
from jax.experimental.pallas import tpu as pltpu
from jax.sharding import PartitionSpec as P

WINDOW = 1024
norm_epsilon = 1e-06
score_scale = 168.0 ** (-0.5)
rope_theta = 10000.0
MESH = pl.DeviceIdType.MESH
TREE = (
    (0, 1, 0, (0, 1)), (0, 2, 0, (0, 1)), (1, 3, 0, (0, 1)), (2, 3, 0, (0, 1)),
    (1, 0, 4, (0, 1)), (2, 0, 4, (0, 1)), (3, 2, 4, (0, 1)), (3, 1, 4, (0, 1)),
    (1, 3, 1, (0,)), (2, 3, 2, (1,)), (3, 2, 2, (0, 1)),
    (1, 0, 2, (0,)), (2, 0, 3, (1,)), (0, 1, 2, (0, 1)),
)
f32 = jnp.float32
bf16 = jnp.bfloat16


def dot(a, b, ca, cb):
    return lax.dot_general(a, b, (((ca,), (cb,)), ((), ())), preferred_element_type=f32)


def rope(n, cosines, sines, half):
    return n * cosines + pltpu.roll(n, half, 1) * sines


def rope_back(g, cosines, sines, half):
    return g * cosines + pltpu.roll(g * sines, half, 1)


def inverse_rms(u):
    return lax.rsqrt(jnp.mean(u * u, axis=-1, keepdims=True) + norm_epsilon)


def norm_rope_back(g, u, gain, cosines, sines, half):
    r = inverse_rms(u)
    w = rope_back(g, cosines, sines, half) * gain
    return r * (w - u * (r * r * jnp.mean(w * u, axis=-1, keepdims=True)))


def axis_of(a, b):
    return 0 if a ^ b == 1 else 1


def children(place, d, w):
    return [(b, d + b - a, axis_of(a, b)) for a, b, e, ws in TREE if (a, e) == (place, d) and w in ws]


def parent(place, d, w):
    (a,) = [(a, e, axis_of(a, b)) for a, b, e, ws in TREE if (b, e + b - a) == (place, d) and w in ws]
    return a


def slot(place, d, axis, w):
    if axis == 2:
        return w
    seen = [(e, axis_of(a, b), v) for a, b, e, ws in TREE if a == place for v in ws]
    return 2 + seen.index((d, axis, w))


SLOTS = 2 + max(sum(len(ws) for a, _, _, ws in TREE if a == place) for place in range(4))


def kernel(
    n_ctx, n_tp, reach, per_kv, kv_count, head, tiles,
    tokens, rgrad, qw, kw, vw, ow, qgain_in, kgain_in, freq_in,
    out_ref, gout_ref,
    wqkv, wo, xg, gg, raw, cos_t, sin_t, q_s, do_s, dot_s, kv_own, halo, e_s, dp_s,
    l_s, ot_s, dqt_s, att, dkv, own_grad, gin, back, part, rs_in, acc, rope_in,
    local_sem, ag_send, ag_recv, f_send, f_recv, b_send, b_recv, rs_send, rs_recv,
):
    c = lax.axis_index("ctx")
    t = lax.axis_index("tp")
    s = lax.rem(c, reach)
    z = lax.div(c, reach)
    nz = n_ctx // reach
    local, width = xg.shape[1], xg.shape[2]
    rows = local * n_tp
    half = head // 2
    qc = kv_count * per_kv * head
    kc = kv_count * head
    qn = per_kv * rows

    barrier = pltpu.get_barrier_semaphore()
    for j in range(1, n_tp):
        pl.semaphore_signal(
            barrier, inc=1, device_id={"tp": lax.rem(t + j, n_tp)}, device_id_type=MESH
        )
    mates = (c + 1 - 2 * lax.rem(s, 2), c + 2 - 4 * lax.div(s, 2))
    for mate in mates:
        pl.semaphore_signal(barrier, inc=1, device_id={"ctx": mate}, device_id_type=MESH)

    @pl.when(z + 1 < nz)
    def _():
        pl.semaphore_signal(barrier, inc=1, device_id={"ctx": c + reach}, device_id_type=MESH)

    @pl.when(z > 0)
    def _():
        pl.semaphore_signal(barrier, inc=1, device_id={"ctx": c - reach}, device_id_type=MESH)

    def local_copy(i, src, dst):
        return pltpu.make_async_copy(src, dst, local_sem.at[i])

    loads = [
        local_copy(0, tokens, xg.at[0]),
        local_copy(1, qw, wqkv.at[:, :qc]),
        local_copy(2, rgrad, gg.at[0]),
        local_copy(3, ow, wo),
    ]
    kv_loads = [
        local_copy(4, kw, wqkv.at[:, qc : qc + kc]),
        local_copy(4, vw, wqkv.at[:, qc + kc : qc + 2 * kc]),
    ]
    table_loads = [local_copy(5, x, rope_in.at[i]) for i, x in enumerate((freq_in, kgain_in, qgain_in))]
    for load in table_loads + loads[:1] + kv_loads + loads[1:]:
        load.start()

    def to_ctx(src, dst, send, recv, target):
        return pltpu.make_async_remote_copy(
            src_ref=src, dst_ref=dst, send_sem=send, recv_sem=recv,
            device_id={"ctx": target}, device_id_type=MESH,
        )

    def to_tp(src, dst, send, recv, target):
        return pltpu.make_async_remote_copy(
            src_ref=src, dst_ref=dst, send_sem=send, recv_sem=recv,
            device_id={"tp": target}, device_id_type=MESH,
        )

    one, none = jnp.int32(1), jnp.int32(0)
    greeted = n_tp - 1 + 2 + jnp.where(z > 0, one, none) + jnp.where(z + 1 < nz, one, none)
    pl.semaphore_wait(barrier, greeted)

    def gather(w, j):
        src, dst = (tokens, xg) if w == 0 else (rgrad, gg)
        return to_tp(src, dst.at[n_tp - j], ag_send, ag_recv.at[w, j - 1],
                     lax.rem(t + j, n_tp))

    for j in range(1, n_tp):
        gather(0, j).start()

    def place(row):
        return lax.rem(t + lax.div(row, local), n_tp) * local + lax.rem(row, local)

    local_copy(5, rope_in, rope_in).wait()
    freq, kgain, qgain = rope_in.at[0], rope_in.at[1], rope_in.at[2]
    fold = rows // 2
    lane = lax.broadcasted_iota(jnp.int32, (fold, head), 1)
    low_lanes = lane < half
    row = lax.broadcasted_iota(jnp.int32, (fold, head), 0) + jnp.where(low_lanes, 0, fold)
    angles = (c * rows + place(row)).astype(f32) * freq[...]
    cosines, sines = jnp.cos(angles), jnp.sin(angles)
    cos_r, sin_r = pltpu.roll(cosines, half, 1), pltpu.roll(sines, half, 1)
    cos_t[:fold, :] = jnp.where(low_lanes, cosines, cos_r)
    cos_t[fold:, :] = jnp.where(low_lanes, cos_r, cosines)
    sin_t[:fold, :] = jnp.where(low_lanes, -sines, sin_r)
    sin_t[fold:, :] = jnp.where(low_lanes, -sin_r, sines)

    spans = (slice(0, local), slice(local, rows))
    chunks = [(w, i) for w in range(2) for i in range(2)]

    def key_values(w, x):
        span = spans[w]
        raw[span, qc : qc + 2 * kc] = dot(x, wqkv[:, qc : qc + 2 * kc], 1, 0)
        for m in range(kv_count):
            u = raw[span, qc + m * head : qc + (m + 1) * head]
            n = u * inverse_rms(u) * kgain[...]
            kv_own[0, m, span] = rope(n, cos_t[span, :], sin_t[span, :], half).astype(bf16)
            v0 = qc + kc + m * head
            kv_own[1, m, span] = raw[span, v0 : v0 + head].astype(bf16)

    def hop(a, b, d, w, i):
        span, e = spans[w], d + b - a
        src = kv_own.at[i, :, span] if d == 0 else halo.at[d - 1, i, :, span]
        return to_ctx(src, halo.at[e - 1, i, :, span], f_send.at[int(d > a)],
                      f_recv.at[e - 1, w, i], c + b - a)

    def ahead(w, i):
        span = spans[w]
        return to_ctx(kv_own.at[i, :, span], halo.at[reach - 1, i, :, span],
                      f_send.at[2], f_recv.at[reach - 1, w, i], c + reach)

    def arrived(d, w, i):
        span = spans[w]
        to_ctx(kv_own.at[i, :, span], halo.at[d - 1, i, :, span], f_send.at[2],
               f_recv.at[d - 1, w, i], c).wait_recv()

    def at(k, a, d):
        return (s == k) & (z > 0) if d > a else s == k

    def relay(jobs):
        for k in range(reach):
            for early in (True, False):
                mine = [j for j in jobs if j[0] == k and (j[1] > k) == early]
                if mine:
                    @pl.when((s == k) & (z > 0) if early else s == k)
                    def _(mine=mine):
                        for a, d, w in mine:
                            for i in range(2):
                                arrived(d, w, i)
                                for b, ws in [(b, ws) for x, b, e, ws in TREE if (x, e) == (a, d)]:
                                    if w in ws:
                                        hop(a, b, d, w, i).start()

    for w in range(2):
        if w == 0:
            loads[0].wait()
            local_copy(4, wqkv.at[:, qc:], wqkv.at[:, qc:]).wait()
            key_values(w, xg[0])
        else:
            for j in range(1, n_tp):
                gather(0, j).wait_recv()
            key_values(w, xg[1:].reshape(rows - local, width))

        @pl.when(z + 1 < nz)
        def _(w=w):
            for i in range(2):
                ahead(w, i).start()

        for k in range(reach - 1):
            @pl.when(s == k)
            def _(k=k, w=w):
                for i in range(2):
                    for b, _, _ in children(k, 0, w):
                        hop(k, b, 0, w, i).start()

    for j in range(1, n_tp):
        gather(1, j).start()
    loads[1].wait()
    raw[:, :qc] = dot(xg[...].reshape(rows, width), wqkv[:, :qc], 1, 0)
    for h in range(kv_count * per_kv):
        m, g = h // per_kv, h % per_kv
        u = raw[:, h * head : (h + 1) * head]
        n = u * inverse_rms(u) * qgain[...]
        q_s[m, g * rows : (g + 1) * rows] = rope(n, cos_t[...], sin_t[...], half).astype(bf16)
    relay([(1, 4, 0), (2, 4, 0), (3, 4, 0), (1, 1, 0), (3, 2, 0)])

    loads[2].wait()
    loads[3].wait()
    for j in range(1, n_tp):
        gather(1, j).wait_recv()
    d_out = dot(gg[...].reshape(rows, width), wo[...], 1, 1).astype(bf16)
    for h in range(kv_count * per_kv):
        m, g = h // per_kv, h % per_kv
        piece = d_out[:, h * head : (h + 1) * head]
        do_s[m, g * rows : (g + 1) * rows] = piece
        dot_s[m, :, g * rows : (g + 1) * rows] = piece.astype(f32).T
    relay([(1, 4, 1), (2, 4, 1), (3, 4, 1), (2, 2, 1), (3, 2, 1)])

    def kv(d, w, m):
        return kv_own[w, m] if isinstance(d, int) and d == 0 else halo[d - 1, w, m]

    def first_pass(d):
        for m in range(kv_count):
            key, value = kv(d, 0, m), kv(d, 1, m)
            e = jnp.exp(dot(key, q_s[m], 1, 1) * score_scale)
            if isinstance(d, int):
                key_row = place(lax.broadcasted_iota(jnp.int32, (rows, 1), 0))
                query_row = place(
                    lax.rem(lax.broadcasted_iota(jnp.int32, (1, qn), 1), jnp.int32(rows))
                )
                keep = query_row >= key_row if d == 0 else query_row < key_row
                e = jnp.where(keep, e, f32(0.0))
            total = jnp.sum(e, axis=0, keepdims=True)
            low = e.astype(bf16)
            e_s[d, m] = low
            mixed = dot(value, low, 0, 0)
            dp_s[d, m] = dot(value, do_s[m], 1, 1) * score_scale
            if isinstance(d, int) and d == 0:
                l_s[m] = total
                ot_s[m] = mixed
            else:
                l_s[m] += total
                ot_s[m] += mixed

    first_pass(0)
    relay([(1, 2, 0), (0, 2, 0)])

    @pl.when(z > 0)
    def _():
        for k in (0,):
            @pl.when(s == k)
            def _():
                for w, i in chunks:
                    arrived(reach, w, i)
        first_pass(reach)

    relay([(2, 3, 1), (0, 2, 1)])

    def pick(*by_place):
        value = jnp.int32(by_place[0])
        for k in range(1, reach):
            value = jnp.where(s == k, jnp.int32(by_place[k]), value)
        return value

    relayed = {(1, 4, 0), (2, 4, 0), (3, 4, 0), (1, 1, 0), (3, 2, 0), (1, 4, 1), (2, 4, 1), (3, 4, 1),
               (2, 2, 1), (3, 2, 1), (1, 2, 0), (0, 2, 0), (2, 3, 1), (0, 2, 1)}
    order = ((3, 2, 1), (1, 2, 3), (2, 1, 3), (1, 2, 3))
    for step in range(reach - 1):
        for k in range(reach):
            d = order[k][step]

            @pl.when((s == k) & (z > 0) if d > k else s == k)
            def _(k=k, d=d):
                for w, i in chunks:
                    if (k, d, w) not in relayed:
                        arrived(d, w, i)

        far = pick(*[order[k][step] for k in range(reach)])

        @pl.when(c >= far)
        def _(far=far):
            first_pass(far)

    inv, delta = [], []
    for m in range(kv_count):
        inv.append(1.0 / l_s[m])
        o_t = (ot_s[m] * inv[m]).astype(bf16).astype(f32)
        delta.append(jnp.sum(o_t * dot_s[m], axis=0, keepdims=True) * score_scale)
        for g in range(per_kv):
            h = m * per_kv + g
            att[:, h * head : (h + 1) * head] = o_t[:, g * rows : (g + 1) * rows].T.astype(bf16)
        dqt_s[m] = jnp.zeros_like(dqt_s[m])

    def second_pass(d, m):
        p = e_s[d, m].astype(f32) * inv[m]
        ds = (p * (dp_s[d, m] - delta[m])).astype(bf16)
        dk = dot(ds, q_s[m], 1, 0)
        dv = dot(p.astype(bf16), do_s[m], 1, 0)
        dqt_s[m] += dot(kv(d, 0, m), ds, 0, 0)
        return dk, dv

    def give(k, d, w, i):
        span = spans[w]
        if d == reach:
            return to_ctx(dkv.at[d - 1, i, :, span], gin.at[0, 2, i, :, span],
                          b_send.at[1], b_recv.at[slot(k, 0, 2, w), i], c - reach)
        a, e, axis = parent(k, d, w)
        return to_ctx(dkv.at[d - 1, i, :, span], gin.at[e, axis, i, :, span],
                      b_send.at[int(d > k)], b_recv.at[slot(a, e, axis, w), i], c + a - k)

    def taken(k, d, axis, w, i):
        span = spans[w]
        to_ctx(dkv.at[0, i, :, span], gin.at[d, axis, i, :, span], b_send.at[0],
               b_recv.at[slot(k, d, axis, w), i], c).wait_recv()
        return gin[d, axis, i, :, span].astype(f32)

    def combine(jobs):
        for k in range(reach):
            for early in (True, False):
                mine = [j for j in jobs if j[0] == k and (j[1] > k) == early]
                if mine:
                    @pl.when((s == k) & (z > 0) if early else s == k)
                    def _(mine=mine):
                        for k, d, w in mine:
                            for i in range(2):
                                span = spans[w]
                                total = dkv[d - 1, i, :, span].astype(f32)
                                for _, _, axis in children(k, d, w):
                                    total += taken(k, d, axis, w, i)
                                dkv[d - 1, i, :, span] = total.astype(bf16)
                                give(k, d, w, i).start()

    for d in (1, 3, 2, 4):
        @pl.when(c >= d)
        def _(d=d):
            for m in range(kv_count):
                dk, dv = second_pass(d, m)
                dkv[d - 1, 0, m] = dk.astype(bf16)
                dkv[d - 1, 1, m] = dv.astype(bf16)
            for k in range(reach):
                leaves = [w for w in (1, 0) if not children(k, d, w)]
                if leaves:
                    @pl.when(s == k)
                    def _(k=k, leaves=leaves):
                        for w in leaves:
                            for i in range(2):
                                give(k, d, w, i).start()

    for m in range(kv_count):
        dk, dv = second_pass(0, m)
        own_grad[0, m] = dk
        own_grad[1, m] = dv

    def rs_copy(w, j, n):
        cols = slice(*tiles[n])
        return to_tp(part.at[w, j, :, cols], rs_in.at[w, j - 1, :, cols], rs_send,
                     rs_recv.at[w, j - 1, n], lax.rem(t + j, n_tp))

    def product(lhs, n, first, last, by_row):
        cols = slice(*tiles[n])
        if by_row:
            return dot(lhs, wo[:, cols], 1, 0)
        return dot(lhs, wqkv[cols, first:last], 1, 1)

    def project(w, lhs, base, first, last, by_row):
        for n, (lo, hi) in enumerate(tiles):
            both = product(lhs, n, first, last, by_row)
            acc[w, :, lo:hi] = base[0, :, lo:hi].astype(f32) + both[:local]
            for j in range(1, n_tp):
                part[w, j, :, lo:hi] = both[j * local : (j + 1) * local].astype(bf16)
                rs_copy(w, j, n).start()

    project(0, att[...], xg, 0, qc, True)
    for m in range(kv_count):
        for g in range(per_kv):
            h = m * per_kv + g
            grad = dqt_s[m, :, g * rows : (g + 1) * rows].T
            u = raw[:, h * head : (h + 1) * head]
            back[:, h * head : (h + 1) * head] = norm_rope_back(
                grad, u, qgain[...], cos_t[...], sin_t[...], half
            ).astype(bf16)
    combine([(0, 2, 1), (0, 2, 0), (2, 3, 1), (2, 2, 1), (3, 2, 1), (3, 2, 0),
             (1, 2, 0), (1, 4, 1), (1, 4, 0), (1, 1, 0)])
    project(1, back[:, :qc], gg, 0, qc, False)
    combine([(2, 4, 1), (2, 4, 0), (3, 4, 1), (3, 4, 0)])

    def landed(w, n):
        lo, hi = tiles[n]
        total = acc[w if w < 2 else 1, :, lo:hi]
        for j in range(1, n_tp):
            rs_copy(w, j, n).wait_recv()
            total += rs_in[w, j - 1, :, lo:hi].astype(f32)
        return total

    for n, (lo, hi) in enumerate(tiles):
        out_ref[:, lo:hi] = landed(0, n).astype(bf16)
    for n, (lo, hi) in enumerate(tiles):
        acc[1, :, lo:hi] = landed(1, n)

    for w in (1, 0):
        span = spans[w]
        for i in range(2):
            for k in range(reach):
                kids = children(k, 0, w)
                if kids:
                    @pl.when(s == k)
                    def _(kids=kids, w=w, i=i, span=span, k=k):
                        for _, _, axis in kids:
                            own_grad[i, :, span] += taken(k, 0, axis, w, i)

            @pl.when(z + 1 < nz)
            def _(w=w, i=i, span=span):
                own_grad[i, :, span] += taken(0, 0, 2, w, i)

        for m in range(kv_count):
            k0 = qc + m * head
            u = raw[span, k0 : k0 + head]
            back[span, k0 : k0 + head] = norm_rope_back(
                own_grad[0, m, span], u, kgain[...], cos_t[span, :], sin_t[span, :], half
            ).astype(bf16)
            back[span, k0 + kc : k0 + kc + head] = own_grad[1, m, span].astype(bf16)

        for n, (lo, hi) in enumerate(tiles):
            piece = product(back[span, qc:], n, qc, qc + 2 * kc, False)
            if w == 0:
                acc[1, :, lo:hi] += piece
            else:
                for j in range(1, n_tp):
                    part[2, j, :, lo:hi] = piece[(j - 1) * local : j * local].astype(bf16)
                    rs_copy(2, j, n).start()
    for n, (lo, hi) in enumerate(tiles):
        gout_ref[:, lo:hi] = landed(2, n).astype(bf16)

    def sent(sem, ref):
        pltpu.make_async_copy(ref, ref, sem).wait()

    sent(ag_send, part.at[:2, 1:])
    sent(rs_send, part.at[:, 1:])

    @pl.when(z + 1 < nz)
    def _():
        sent(f_send.at[2], kv_own)

    for k in range(reach):
        for early in (True, False):
            @pl.when((s == k) & (z > 0) if early else s == k)
            def _(k=k, early=early):
                halves = sum(len(ws) for a, b, d, ws in TREE if a == k and (d > k) == early)
                if halves // 2:
                    sent(f_send.at[int(early)], halo.at[: halves // 2])
                if halves % 2:
                    sent(f_send.at[int(early)], halo.at[0, :, :, spans[0]])
                first, last = (k, reach) if early else (0, k)
                if first < last:
                    sent(b_send.at[int(early)], dkv.at[first:last])


def write(a, b, a_out, b_out, sems):
    split = sems.shape[1]
    step = a.shape[0] // split
    copies = [
        pltpu.make_async_copy(x.at[pl.ds(i * step, step)], y.at[pl.ds(i * step, step)], sems.at[w, i])
        for w, (x, y) in enumerate(((a, a_out), (b, b_out)))
        for i in range(split)
    ]
    for copy in copies:
        copy.start()
    for copy in copies:
        copy.wait()


def on_device(
    tokens, result_grad, query_weight, key_weight, value_weight, output_weight, query_gain, key_gain
):
    n_ctx = lax.axis_size("ctx")
    n_tp = lax.axis_size("tp")
    local, width = tokens.shape
    rows = local * n_tp
    head = query_gain.shape[0]
    kv_count = key_weight.shape[1] // head
    per_kv = query_weight.shape[1] // key_weight.shape[1]
    reach = WINDOW // rows
    assert reach == 4 and n_ctx % reach == 0
    qc = kv_count * per_kv * head
    kc = kv_count * head
    qn = per_kv * rows
    tiles = tuple((lo, min(lo + 1024, width)) for lo in range(0, width, 1024))
    exponent = np.arange(head // 2, dtype=np.float32) * np.float32(2.0 / head)
    frequency = np.power(np.float32(rope_theta), -exponent)
    frequency = jnp.asarray(np.concatenate([frequency, frequency])[None, :])
    any_spec = pl.BlockSpec(memory_space=pl.ANY)
    vmem_spec = pl.BlockSpec(memory_space=pltpu.VMEM)
    block = (2, kv_count, rows, head)
    dma = pltpu.SemaphoreType.DMA
    out = pltpu.VMEM((local, width), bf16)
    layer_output, tokens_grad = pl.pallas_call(
        functools.partial(kernel, n_ctx, n_tp, reach, per_kv, kv_count, head, tiles),
        out_shape=(out, out),
        in_specs=[any_spec] * 9,
        out_specs=(vmem_spec, vmem_spec),
        scratch_shapes=[
            pltpu.VMEM((width, qc + 2 * kc), bf16),
            pltpu.VMEM((qc, width), bf16),
            pltpu.VMEM((n_tp, local, width), bf16),
            pltpu.VMEM((n_tp, local, width), bf16),
            pltpu.VMEM((rows, qc + 2 * kc), f32),
            pltpu.VMEM((rows, head), f32),
            pltpu.VMEM((rows, head), f32),
            pltpu.VMEM((kv_count, qn, head), bf16),
            pltpu.VMEM((kv_count, qn, head), bf16),
            pltpu.VMEM((kv_count, head, qn), f32),
            pltpu.VMEM(block, bf16),
            pltpu.VMEM((reach,) + block, bf16),
            pltpu.VMEM((reach + 1, kv_count, rows, qn), bf16),
            pltpu.VMEM((reach + 1, kv_count, rows, qn), f32),
            pltpu.VMEM((kv_count, 1, qn), f32),
            pltpu.VMEM((kv_count, head, qn), f32),
            pltpu.VMEM((kv_count, head, qn), f32),
            pltpu.VMEM((rows, qc), bf16),
            pltpu.VMEM((reach,) + block, bf16),
            pltpu.VMEM(block, f32),
            pltpu.VMEM((reach + 1, 3) + block, bf16),
            pltpu.VMEM((rows, qc + 2 * kc), bf16),
            pltpu.VMEM((3, n_tp, local, width), bf16),
            pltpu.VMEM((3, n_tp - 1, local, width), bf16),
            pltpu.VMEM((2, local, width), f32),
            pltpu.VMEM((3, 1, head), f32),
            dma((6,)),
            dma,
            dma((2, n_tp - 1)),
            dma((3,)),
            dma((reach, 2, 2)),
            dma((2,)),
            dma((SLOTS, 2)),
            dma,
            dma((3, n_tp - 1, len(tiles))),
        ],
        compiler_params=pltpu.CompilerParams(
            collective_id=0, has_side_effects=True, vmem_limit_bytes=56 * 1024 * 1024
        ),
    )(
        tokens, result_grad, query_weight, key_weight, value_weight, output_weight,
        query_gain[None, :], key_gain[None, :], frequency,
    )
    result = jax.ShapeDtypeStruct((local, width), bf16)
    return pl.pallas_call(
        write,
        out_shape=(result, result),
        in_specs=[vmem_spec] * 2,
        out_specs=(any_spec, any_spec),
        scratch_shapes=[dma((2, 4 if local % 64 == 0 else 1))],
        compiler_params=pltpu.CompilerParams(vmem_limit_bytes=2 * 1024 * 1024),
    )(layer_output, tokens_grad)


def solution(mesh):
    in_specs = (
        P(("ctx", "tp"), None),
        P(("ctx", "tp"), None),
        P(None, "tp"),
        P(None, "tp"),
        P(None, "tp"),
        P("tp", None),
        P(),
        P(),
    )
    out_specs = (P(("ctx", "tp"), None), P(("ctx", "tp"), None))
    return jax.shard_map(
        on_device, mesh=mesh, in_specs=in_specs, out_specs=out_specs, check_vma=False
    )
```

```python
import functools

import jax
import jax.numpy as jnp
import numpy as np
from jax import lax
from jax.experimental import pallas as pl
from jax.experimental.pallas import tpu as pltpu
from jax.sharding import PartitionSpec as P

WINDOW = 1024
norm_epsilon = 1e-06
score_scale = 168.0 ** (-0.5)
rope_theta = 10000.0
MESH = pl.DeviceIdType.MESH
TREE = (
    (0, 1, 0, (0, 1)), (0, 2, 0, (0, 1)), (1, 3, 0, (0, 1)), (2, 3, 0, (0, 1)),
    (1, 0, 4, (0, 1)), (2, 0, 4, (0, 1)), (3, 2, 4, (0, 1)), (3, 1, 4, (0, 1)),
    (1, 3, 1, (0,)), (2, 3, 2, (1,)), (3, 2, 2, (0, 1)),
    (1, 0, 2, (0,)), (2, 0, 3, (1,)), (0, 1, 2, (0, 1)),
)
OUT = (
    (0, 0, 1, 0, 0), (1, 3, 0, 0, 0), (2, 3, 0, 0, 0), (1, 1, 1, 0, 0), (0, 2, 0, 0, 0),
    (3, 2, 1, 0, 0), (1, 2, 0, 0, 0), (1, 0, 1, 0, 0), (0, 1, 0, 0, 0), (2, 0, 1, 0, 0),
    (0, 2, 0, 0, 1), (0, 1, 0, 0, 1), (2, 3, 0, 0, 1), (1, 0, 1, 0, 1), (0, 0, 1, 0, 1),
    (3, 1, 1, 0, 1), (1, 1, 1, 0, 1), (2, 0, 1, 0, 1), (2, 2, 1, 0, 1), (1, 3, 0, 0, 1),
    (3, 2, 1, 0, 1), (3, 3, 1, 0, 1), (1, 3, 0, 1, 0), (2, 0, 0, 3, 0), (2, 1, 0, 3, 0),
    (0, 1, 0, 2, 0), (0, 2, 0, 2, 0), (2, 3, 0, 3, 0), (1, 3, 0, 1, 1), (3, 2, 0, 2, 1),
    (0, 1, 0, 2, 1), (1, 0, 0, 2, 1),
)
HOME = (
    (1, 0, 0, 3, 1), (3, 3, -1, 4, 0), (3, 0, 0, 3, 0), (1, 1, -1, 4, 0), (0, 2, 0, 1, 1),
    (3, 2, 0, 1, 1), (0, 0, -1, 4, 1), (0, 1, 0, 3, 1), (2, 3, -1, 3, 1), (2, 1, 0, 1, 1),
    (1, 0, 0, 1, 0), (2, 3, 0, 1, 0), (3, 1, 0, 2, 0), (0, 0, -1, 4, 0), (1, 0, 0, 1, 1),
    (3, 1, 0, 2, 1), (2, 2, -1, 4, 0), (0, 1, 0, 3, 0), (3, 2, 0, 1, 0), (1, 1, -1, 4, 1),
    (3, 2, 0, 4, 1), (0, 2, -1, 2, 0), (0, 2, 0, 1, 0), (0, 2, -1, 2, 1), (1, 0, 0, 3, 0),
    (2, 3, -1, 3, 0), (1, 3, -1, 2, 1), (2, 0, 0, 2, 0), (1, 3, -1, 2, 0), (2, 2, -1, 4, 1),
    (3, 1, 0, 3, 1), (2, 0, 0, 2, 1),
)
PASS_ON = (
    (), ((1, 1, 0), (0, 2, 0), (2, 3, 0)), ((1, 1, 1), (3, 2, 1)), ((0, 2, 1), (1, 2, 1)), (),
)
ADD_UP = (
    (), (), ((0, 2, 1), (2, 3, 1)), ((1, 4, 1), (0, 2, 0)), ((1, 1, 1), (2, 3, 0), (3, 2, 0), (1, 4, 0)),
)
FIRST = ((4, 2, 3, 1), (1, 2, 4, 3), (2, 3, 4, 1), (2, 1, 4, 3))
SECOND = ((4, 1, 3, 2), (3, 2, 1, 4), (4, 1, 2, 3), (4, 3, 1, 2))
GROUP = 4
f32 = jnp.float32
bf16 = jnp.bfloat16


def dot(a, b, ca, cb):
    return lax.dot_general(a, b, (((ca,), (cb,)), ((), ())), preferred_element_type=f32)


def rope(n, cosines, sines, half):
    return n * cosines + pltpu.roll(n, half, 1) * sines


def rope_back(g, cosines, sines, half):
    return g * cosines + pltpu.roll(g * sines, half, 1)


def inverse_rms(u):
    return lax.rsqrt(jnp.mean(u * u, axis=-1, keepdims=True) + norm_epsilon)


def norm_rope_back(g, u, gain, cosines, sines, half):
    r = inverse_rms(u)
    w = rope_back(g, cosines, sines, half) * gain
    return r * (w - u * (r * r * jnp.mean(w * u, axis=-1, keepdims=True)))


def axis_of(a, b):
    return 0 if a ^ b == 1 else 1


def children(place, d, w):
    return [(b, d + b - a, axis_of(a, b)) for a, b, e, ws in TREE if (a, e) == (place, d) and w in ws]


def parent(place, d, w):
    (a,) = [(a, e, axis_of(a, b)) for a, b, e, ws in TREE if (b, e + b - a) == (place, d) and w in ws]
    return a


def slot(place, d, axis, w):
    if axis == 2:
        return w
    seen = [(e, axis_of(a, b), v) for a, b, e, ws in TREE if a == place for v in ws]
    return 2 + seen.index((d, axis, w))


SLOTS = 2 + max(sum(len(ws) for a, _, _, ws in TREE if a == place) for place in range(4))


def step_of(a, b, ahead):
    return GROUP * ahead + b - a


def out_of(place, d, w):
    return [(b, g) for a, b, g, e, v in OUT if (a, e, v) == (place, d, w)]


def home_of(place, d, w):
    ((b, g),) = [(b, g) for a, b, g, e, v in HOME if (a, e, v) == (place, d, w)]
    return b, g


def inbound(place):
    return [(a, e, g, v) for a, b, g, e, v in HOME if b == place]


def givers(place, d, w):
    return [
        (a, e, g) for a, e, g, v in inbound(place)
        if v == w and e + step_of(a, place, g) == d
    ]


def partners(place, g):
    pairs = {(a, b, h) for a, b, h, _, _ in OUT + HOME}
    pairs |= {(b, a, -h) for a, b, h in pairs}
    return sorted(b for a, b, h in pairs if (a, h) == (place, g) and (b, g) != (place, 0))


SLOTS = max(len(inbound(place)) for place in range(GROUP))


def kernel(
    n_ctx, n_tp, reach, per_kv, kv_count, head, tiles,
    tokens, rgrad, qw, kw, vw, ow, qgain_in, kgain_in, freq_in,
    out_ref, gout_ref,
    wqkv, wo, xg, gg, raw, cos_t, sin_t, q_s, do_s, dot_s, kv_own, halo, e_s, dp_s,
    l_s, ot_s, dqt_s, att, dkv, own_grad, gin, back, part, rs_in, acc, rope_in,
    local_sem, ag_send, ag_recv, f_send, f_recv, b_send, b_recv, rs_send, rs_recv,
):
    c = lax.axis_index("ctx")
    t = lax.axis_index("tp")
    s = lax.rem(c, reach)
    z = lax.div(c, reach)
    nz = n_ctx // reach
    local, width = xg.shape[1], xg.shape[2]
    rows = local * n_tp
    half = head // 2
    qc = kv_count * per_kv * head
    kc = kv_count * head
    qn = per_kv * rows

    barrier = pltpu.get_barrier_semaphore()
    for j in range(1, n_tp):
        pl.semaphore_signal(
            barrier, inc=1, device_id={"tp": lax.rem(t + j, n_tp)}, device_id_type=MESH
        )
    def here(k, early=False, later=False):
        on = s == k
        if early:
            on = on & (z > 0)
        if later:
            on = on & (z + 1 < nz)
        return on

    def pick(by_place):
        value = jnp.int32(by_place[0])
        for k in range(1, reach):
            value = jnp.where(s == k, jnp.int32(by_place[k]), value)
        return value

    for k in range(reach):
        for g in (-1, 0, 1):
            if partners(k, g):
                @pl.when(here(k, early=g < 0, later=g > 0))
                def _(k=k, g=g):
                    for b in partners(k, g):
                        pl.semaphore_signal(
                            barrier, inc=1, device_id={"ctx": c + step_of(k, b, g)},
                            device_id_type=MESH,
                        )

    def local_copy(i, src, dst):
        return pltpu.make_async_copy(src, dst, local_sem.at[i])

    loads = [
        local_copy(0, tokens, xg.at[0]),
        local_copy(1, qw, wqkv.at[:, :qc]),
        local_copy(2, rgrad, gg.at[0]),
        local_copy(3, ow, wo),
    ]
    kv_loads = [
        local_copy(4, kw, wqkv.at[:, qc : qc + kc]),
        local_copy(4, vw, wqkv.at[:, qc + kc : qc + 2 * kc]),
    ]
    table_loads = [local_copy(5, x, rope_in.at[i]) for i, x in enumerate((freq_in, kgain_in, qgain_in))]
    for load in table_loads + loads[:1] + kv_loads + loads[1:]:
        load.start()

    def to_ctx(src, dst, send, recv, target):
        return pltpu.make_async_remote_copy(
            src_ref=src, dst_ref=dst, send_sem=send, recv_sem=recv,
            device_id={"ctx": target}, device_id_type=MESH,
        )

    def to_tp(src, dst, send, recv, target):
        return pltpu.make_async_remote_copy(
            src_ref=src, dst_ref=dst, send_sem=send, recv_sem=recv,
            device_id={"tp": target}, device_id_type=MESH,
        )

    count = [[len(partners(k, g)) for k in range(reach)] for g in (-1, 0, 1)]
    none = jnp.int32(0)
    greeted = (
        n_tp - 1
        + jnp.where(z > 0, pick(count[0]), none)
        + pick(count[1])
        + jnp.where(z + 1 < nz, pick(count[2]), none)
    )
    def place(row):
        return lax.rem(t + lax.div(row, local), n_tp) * local + lax.rem(row, local)

    local_copy(5, rope_in, rope_in).wait()
    freq, kgain, qgain = rope_in.at[0], rope_in.at[1], rope_in.at[2]
    fold = rows // 2
    lane = lax.broadcasted_iota(jnp.int32, (fold, head), 1)
    low_lanes = lane < half
    row = lax.broadcasted_iota(jnp.int32, (fold, head), 0) + jnp.where(low_lanes, 0, fold)
    angles = (c * rows + place(row)).astype(f32) * freq[...]
    cosines, sines = jnp.cos(angles), jnp.sin(angles)
    cos_r, sin_r = pltpu.roll(cosines, half, 1), pltpu.roll(sines, half, 1)
    cos_t[:fold, :] = jnp.where(low_lanes, cosines, cos_r)
    cos_t[fold:, :] = jnp.where(low_lanes, cos_r, cosines)
    sin_t[:fold, :] = jnp.where(low_lanes, -sines, sin_r)
    sin_t[fold:, :] = jnp.where(low_lanes, -sin_r, sines)

    pl.semaphore_wait(barrier, greeted)

    cuts = (0, width // 256 * 128, width)

    def gather(w, j, n):
        src, dst = (tokens, xg) if w == 0 else (rgrad, gg)
        cols = slice(cuts[n], cuts[n + 1])
        return to_tp(src.at[:, cols], dst.at[n_tp - j, :, cols], ag_send,
                     ag_recv.at[w, j - 1, n], lax.rem(t + j, n_tp))

    for w in range(2):
        for n in range(2):
            for j in range(1, n_tp):
                gather(w, j, n).start()

    spans = (slice(0, local), slice(local, rows))
    chunks = [(w, i) for w in range(2) for i in range(2)]

    def key_values(w, x):
        span = spans[w]
        raw[span, qc : qc + 2 * kc] = x
        for m in range(kv_count):
            u = raw[span, qc + m * head : qc + (m + 1) * head]
            n = u * inverse_rms(u) * kgain[...]
            kv_own[0, m, span] = rope(n, cos_t[span, :], sin_t[span, :], half).astype(bf16)
            v0 = qc + kc + m * head
            kv_own[1, m, span] = raw[span, v0 : v0 + head].astype(bf16)

    def hop(a, b, g, d, w, i):
        span, e = spans[w], d + step_of(a, b, g)
        src = kv_own.at[i, :, span] if d == 0 else halo.at[d - 1, i, :, span]
        kind = 2 if g else int(d > a)
        return to_ctx(src, halo.at[e - 1, i, :, span], f_send.at[kind],
                      f_recv.at[e - 1, w, i], c + step_of(a, b, g))

    def arrived(d, w, i):
        span = spans[w]
        to_ctx(kv_own.at[i, :, span], halo.at[d - 1, i, :, span], f_send.at[2],
               f_recv.at[d - 1, w, i], c).wait_recv()

    settled = set()

    def settle(jobs):
        for k, d, w in jobs:
            if (k, d, w) in settled:
                continue
            settled.add((k, d, w))

            @pl.when(here(k, early=d > k))
            def _(k=k, d=d, w=w):
                for i in range(2):
                    arrived(d, w, i)
                    for b, g in out_of(k, d, w):
                        hop(k, b, g, d, w, i).start()

    for w in range(2):
        if w == 0:
            loads[0].wait()
            local_copy(4, wqkv.at[:, qc:], wqkv.at[:, qc:]).wait()
            key_values(w, dot(xg[0], wqkv[:, qc:], 1, 0))
        else:
            projected = None
            for n in range(2):
                cols = slice(cuts[n], cuts[n + 1])
                for j in range(1, n_tp):
                    gather(0, j, n).wait_recv()
                x = xg[1:, :, cols].reshape(rows - local, cuts[n + 1] - cuts[n])
                piece = dot(x, wqkv[cols, qc:], 1, 0)
                projected = piece if n == 0 else projected + piece
            key_values(w, projected)

        for k in range(reach):
            for ahead in (1, 0):
                targets = [b for b, g in out_of(k, 0, w) if g == ahead]
                if targets:
                    @pl.when(here(k, later=ahead > 0))
                    def _(k=k, w=w, ahead=ahead, targets=targets):
                        for b in targets:
                            for i in range(2):
                                hop(k, b, ahead, 0, w, i).start()

    loads[1].wait()
    raw[:, :qc] = dot(xg[...].reshape(rows, width), wqkv[:, :qc], 1, 0)
    for h in range(kv_count * per_kv):
        m, g = h // per_kv, h % per_kv
        u = raw[:, h * head : (h + 1) * head]
        n = u * inverse_rms(u) * qgain[...]
        q_s[m, g * rows : (g + 1) * rows] = rope(n, cos_t[...], sin_t[...], half).astype(bf16)
    settle(PASS_ON[0])

    loads[2].wait()
    loads[3].wait()
    for j in range(1, n_tp):
        for n in range(2):
            gather(1, j, n).wait_recv()
    d_out = dot(gg[...].reshape(rows, width), wo[...], 1, 1).astype(bf16)
    for h in range(kv_count * per_kv):
        m, g = h // per_kv, h % per_kv
        piece = d_out[:, h * head : (h + 1) * head]
        do_s[m, g * rows : (g + 1) * rows] = piece
        dot_s[m, :, g * rows : (g + 1) * rows] = piece.astype(f32).T
    settle(PASS_ON[1])

    def kv(d, w, m):
        return kv_own[w, m] if isinstance(d, int) and d == 0 else halo[d - 1, w, m]

    def first_pass(d):
        for m in range(kv_count):
            key, value = kv(d, 0, m), kv(d, 1, m)
            e = jnp.exp(dot(key, q_s[m], 1, 1) * score_scale)
            key_row = place(lax.broadcasted_iota(jnp.int32, (rows, 1), 0))
            query_row = place(
                lax.rem(lax.broadcasted_iota(jnp.int32, (1, qn), 1), jnp.int32(rows))
            )
            if isinstance(d, int):
                keep = query_row >= key_row
            else:
                keep = query_row < key_row + jnp.where(d == reach, 0, rows)
            e = jnp.where(keep, e, f32(0.0))
            total = jnp.sum(e, axis=0, keepdims=True)
            low = e.astype(bf16)
            e_s[d, m] = low
            mixed = dot(value, low, 0, 0)
            dp_s[d, m] = dot(value, do_s[m], 1, 1) * score_scale
            if isinstance(d, int) and d == 0:
                l_s[m] = total
                ot_s[m] = mixed
            else:
                l_s[m] += total
                ot_s[m] += mixed

    first_pass(0)

    settle(PASS_ON[2])
    for step in range(reach):
        for k in range(reach):
            settle([(k, FIRST[k][step], w) for w in range(2)])
        far = pick([order[step] for order in FIRST])

        @pl.when(c >= far)
        def _(far=far):
            first_pass(far)

        if step < 2:
            settle(PASS_ON[3 + step])

    inv, delta = [], []
    for m in range(kv_count):
        inv.append(1.0 / l_s[m])
        o_t = (ot_s[m] * inv[m]).astype(bf16).astype(f32)
        delta.append(jnp.sum(o_t * dot_s[m], axis=0, keepdims=True) * score_scale)
        for g in range(per_kv):
            h = m * per_kv + g
            att[:, h * head : (h + 1) * head] = o_t[:, g * rows : (g + 1) * rows].T.astype(bf16)
        dqt_s[m] = jnp.zeros_like(dqt_s[m])

    def second_pass(d, m):
        p = e_s[d, m].astype(f32) * inv[m]
        ds = (p * (dp_s[d, m] - delta[m])).astype(bf16)
        dk = dot(ds, q_s[m], 1, 0)
        dv = dot(p.astype(bf16), do_s[m], 1, 0)
        dqt_s[m] += dot(kv(d, 0, m), ds, 0, 0)
        return dk, dv

    def give(k, d, w, i):
        span = spans[w]
        b, g = home_of(k, d, w)
        n = inbound(b).index((k, d, g, w))
        return to_ctx(dkv.at[d - 1, i, :, span], gin.at[n, i, :, span],
                      b_send.at[int(d > k)], b_recv.at[n, i], c + step_of(k, b, g))

    def taken(k, giver, w, i):
        span = spans[w]
        n = inbound(k).index((*giver, w))
        to_ctx(dkv.at[0, i, :, span], gin.at[n, i, :, span], b_send.at[0],
               b_recv.at[n, i], c).wait_recv()
        return gin[n, i, :, span].astype(f32)

    def combine(jobs):
        for k, d, w in jobs:
            @pl.when(here(k, early=d > k))
            def _(k=k, d=d, w=w):
                span = spans[w]
                for i in range(2):
                    total = dkv[d - 1, i, :, span].astype(f32)
                    for giver in givers(k, d, w):
                        total += taken(k, giver, w, i)
                    dkv[d - 1, i, :, span] = total.astype(bf16)
                    give(k, d, w, i).start()

    for step in range(reach):
        far = pick([order[step] for order in SECOND])

        @pl.when(c >= far)
        def _(step=step, far=far):
            for m in range(kv_count):
                dk, dv = second_pass(far, m)
                dkv[far - 1, 0, m] = dk.astype(bf16)
                dkv[far - 1, 1, m] = dv.astype(bf16)
            for k in range(reach):
                d = SECOND[k][step]
                leaves = [v for a, _, _, e, v in HOME if (a, e) == (k, d) and not givers(k, d, v)]
                if leaves:
                    @pl.when(here(k))
                    def _(k=k, d=d, leaves=leaves):
                        for w in leaves:
                            for i in range(2):
                                give(k, d, w, i).start()

    for m in range(kv_count):
        dk, dv = second_pass(0, m)
        own_grad[0, m] = dk
        own_grad[1, m] = dv

    def rs_copy(w, j, n):
        cols = slice(*tiles[n])
        return to_tp(part.at[w, j, :, cols], rs_in.at[w, j - 1, :, cols], rs_send,
                     rs_recv.at[w, j - 1, n], lax.rem(t + j, n_tp))

    def product(lhs, n, first, last, by_row):
        cols = slice(*tiles[n])
        if by_row:
            return dot(lhs, wo[:, cols], 1, 0)
        return dot(lhs, wqkv[cols, first:last], 1, 1)

    def project(w, lhs, base, first, last, by_row):
        for n, (lo, hi) in enumerate(tiles):
            both = product(lhs, n, first, last, by_row)
            acc[w, :, lo:hi] = base[0, :, lo:hi].astype(f32) + both[:local]
            for j in range(1, n_tp):
                part[w, j, :, lo:hi] = both[j * local : (j + 1) * local].astype(bf16)
                rs_copy(w, j, n).start()

    combine(ADD_UP[0])
    project(0, att[...], xg, 0, qc, True)
    combine(ADD_UP[1])
    for m in range(kv_count):
        for g in range(per_kv):
            h = m * per_kv + g
            grad = dqt_s[m, :, g * rows : (g + 1) * rows].T
            u = raw[:, h * head : (h + 1) * head]
            back[:, h * head : (h + 1) * head] = norm_rope_back(
                grad, u, qgain[...], cos_t[...], sin_t[...], half
            ).astype(bf16)
    combine(ADD_UP[2])
    project(1, back[:, :qc], gg, 0, qc, False)
    combine(ADD_UP[3])
    def landed(w, n):
        lo, hi = tiles[n]
        total = acc[w if w < 2 else 1, :, lo:hi]
        for j in range(1, n_tp):
            rs_copy(w, j, n).wait_recv()
            total += rs_in[w, j - 1, :, lo:hi].astype(f32)
        return total

    for n, (lo, hi) in enumerate(tiles):
        out_ref[:, lo:hi] = landed(0, n).astype(bf16)
    combine(ADD_UP[4])
    for n, (lo, hi) in enumerate(tiles):
        acc[1, :, lo:hi] = landed(1, n)

    for w in (1, 0):
        span = spans[w]
        for i in range(2):
            for k in range(reach):
                for later in (False, True):
                    mine = [x for x in givers(k, 0, w) if bool(x[2]) == later]
                    if mine:
                        @pl.when(here(k, later=later))
                        def _(k=k, mine=mine, w=w, i=i, span=span):
                            for giver in mine:
                                own_grad[i, :, span] += taken(k, giver, w, i)

        for m in range(kv_count):
            k0 = qc + m * head
            u = raw[span, k0 : k0 + head]
            back[span, k0 : k0 + head] = norm_rope_back(
                own_grad[0, m, span], u, kgain[...], cos_t[span, :], sin_t[span, :], half
            ).astype(bf16)
            back[span, k0 + kc : k0 + kc + head] = own_grad[1, m, span].astype(bf16)

        for n, (lo, hi) in enumerate(tiles):
            piece = product(back[span, qc:], n, qc, qc + 2 * kc, False)
            if w == 0:
                acc[1, :, lo:hi] += piece
            else:
                for j in range(1, n_tp):
                    part[2, j, :, lo:hi] = piece[(j - 1) * local : j * local].astype(bf16)
                    rs_copy(2, j, n).start()
    for n, (lo, hi) in enumerate(tiles):
        gout_ref[:, lo:hi] = landed(2, n).astype(bf16)

    def sent(sem, ref):
        pltpu.make_async_copy(ref, ref, sem).wait()

    sent(ag_send, part.at[:2, 1:])
    sent(rs_send, part.at[:, 1:])

    def drain(sem, ref, pieces):
        few = [pieces.count(w) for w in range(2)]
        both = min(few)
        if both:
            sent(sem, ref.at[:both])
        for w in range(2):
            if few[w] > both:
                sent(sem, ref.at[: few[w] - both, :, :, spans[w]])

    for k in range(reach):
        for kind in range(3):
            gone = [v for a, b, g, e, v in OUT if a == k and kind == (2 if g else int(e > a))]
            back_gone = [v for a, b, g, e, v in HOME if a == k and kind == int(e > a)]
            if gone or back_gone:
                @pl.when(here(k, early=kind == 1, later=kind == 2))
                def _(kind=kind, gone=gone, back_gone=back_gone):
                    drain(f_send.at[kind], halo, gone)
                    if kind < 2:
                        drain(b_send.at[kind], dkv, back_gone)


def write(a, b, a_out, b_out, sems):
    split = sems.shape[1]
    step = a.shape[0] // split
    copies = [
        pltpu.make_async_copy(x.at[pl.ds(i * step, step)], y.at[pl.ds(i * step, step)], sems.at[w, i])
        for w, (x, y) in enumerate(((a, a_out), (b, b_out)))
        for i in range(split)
    ]
    for copy in copies:
        copy.start()
    for copy in copies:
        copy.wait()


def on_device(
    tokens, result_grad, query_weight, key_weight, value_weight, output_weight, query_gain, key_gain
):
    n_ctx = lax.axis_size("ctx")
    n_tp = lax.axis_size("tp")
    local, width = tokens.shape
    rows = local * n_tp
    head = query_gain.shape[0]
    kv_count = key_weight.shape[1] // head
    per_kv = query_weight.shape[1] // key_weight.shape[1]
    reach = WINDOW // rows
    assert reach == GROUP and n_ctx % reach == 0
    qc = kv_count * per_kv * head
    kc = kv_count * head
    qn = per_kv * rows
    tiles = tuple((lo, min(lo + 1024, width)) for lo in range(0, width, 1024))
    exponent = np.arange(head // 2, dtype=np.float32) * np.float32(2.0 / head)
    frequency = np.power(np.float32(rope_theta), -exponent)
    frequency = jnp.asarray(np.concatenate([frequency, frequency])[None, :])
    any_spec = pl.BlockSpec(memory_space=pl.ANY)
    vmem_spec = pl.BlockSpec(memory_space=pltpu.VMEM)
    block = (2, kv_count, rows, head)
    dma = pltpu.SemaphoreType.DMA
    out = pltpu.VMEM((local, width), bf16)
    layer_output, tokens_grad = pl.pallas_call(
        functools.partial(kernel, n_ctx, n_tp, reach, per_kv, kv_count, head, tiles),
        out_shape=(out, out),
        in_specs=[any_spec] * 9,
        out_specs=(vmem_spec, vmem_spec),
        scratch_shapes=[
            pltpu.VMEM((width, qc + 2 * kc), bf16),
            pltpu.VMEM((qc, width), bf16),
            pltpu.VMEM((n_tp, local, width), bf16),
            pltpu.VMEM((n_tp, local, width), bf16),
            pltpu.VMEM((rows, qc + 2 * kc), f32),
            pltpu.VMEM((rows, head), f32),
            pltpu.VMEM((rows, head), f32),
            pltpu.VMEM((kv_count, qn, head), bf16),
            pltpu.VMEM((kv_count, qn, head), bf16),
            pltpu.VMEM((kv_count, head, qn), f32),
            pltpu.VMEM(block, bf16),
            pltpu.VMEM((reach,) + block, bf16),
            pltpu.VMEM((reach + 1, kv_count, rows, qn), bf16),
            pltpu.VMEM((reach + 1, kv_count, rows, qn), f32),
            pltpu.VMEM((kv_count, 1, qn), f32),
            pltpu.VMEM((kv_count, head, qn), f32),
            pltpu.VMEM((kv_count, head, qn), f32),
            pltpu.VMEM((rows, qc), bf16),
            pltpu.VMEM((reach,) + block, bf16),
            pltpu.VMEM(block, f32),
            pltpu.VMEM((SLOTS,) + block, bf16),
            pltpu.VMEM((rows, qc + 2 * kc), bf16),
            pltpu.VMEM((3, n_tp, local, width), bf16),
            pltpu.VMEM((3, n_tp - 1, local, width), bf16),
            pltpu.VMEM((2, local, width), f32),
            pltpu.VMEM((3, 1, head), f32),
            dma((6,)),
            dma,
            dma((2, n_tp - 1, 2)),
            dma((3,)),
            dma((reach, 2, 2)),
            dma((2,)),
            dma((SLOTS, 2)),
            dma,
            dma((3, n_tp - 1, len(tiles))),
        ],
        compiler_params=pltpu.CompilerParams(
            collective_id=0, has_side_effects=True, vmem_limit_bytes=56 * 1024 * 1024
        ),
    )(
        tokens, result_grad, query_weight, key_weight, value_weight, output_weight,
        query_gain[None, :], key_gain[None, :], frequency,
    )
    result = jax.ShapeDtypeStruct((local, width), bf16)
    return pl.pallas_call(
        write,
        out_shape=(result, result),
        in_specs=[vmem_spec] * 2,
        out_specs=(any_spec, any_spec),
        scratch_shapes=[dma((2, 4 if local % 64 == 0 else 1))],
        compiler_params=pltpu.CompilerParams(vmem_limit_bytes=2 * 1024 * 1024),
    )(layer_output, tokens_grad)


def solution(mesh):
    in_specs = (
        P(("ctx", "tp"), None),
        P(("ctx", "tp"), None),
        P(None, "tp"),
        P(None, "tp"),
        P(None, "tp"),
        P("tp", None),
        P(),
        P(),
    )
    out_specs = (P(("ctx", "tp"), None), P(("ctx", "tp"), None))
    return jax.shard_map(
        on_device, mesh=mesh, in_specs=in_specs, out_specs=out_specs, check_vma=False
    )
```

```python
import functools

import jax
import jax.numpy as jnp
import numpy as np
from jax import lax
from jax.experimental import pallas as pl
from jax.experimental.pallas import tpu as pltpu
from jax.sharding import PartitionSpec as P

WINDOW = 1024
norm_epsilon = 1e-06
score_scale = 168.0 ** (-0.5)
rope_theta = 10000.0
MESH = pl.DeviceIdType.MESH
OUT = (
    (0, 0, 1, 0, 0, 0), (0, 0, 1, 0, 0, 1), (1, 3, 0, 0, 0, 0), (1, 3, 0, 0, 0, 1), (2, 3, 0, 0, 0, 0),
    (2, 3, 0, 0, 0, 1), (1, 1, 1, 0, 0, 0), (1, 1, 1, 0, 0, 1), (0, 2, 0, 0, 0, 0), (0, 2, 0, 0, 0, 1),
    (3, 2, 1, 0, 0, 0), (3, 2, 1, 0, 0, 1), (1, 2, 0, 0, 0, 0), (1, 2, 0, 0, 0, 1), (1, 0, 1, 0, 0, 0),
    (1, 0, 1, 0, 0, 1), (0, 1, 0, 0, 0, 0), (0, 1, 0, 0, 0, 1), (2, 0, 1, 0, 0, 0), (2, 0, 1, 0, 0, 1),
    (0, 2, 0, 0, 1, 0), (0, 2, 0, 0, 1, 1), (0, 1, 0, 0, 1, 0), (0, 1, 0, 0, 1, 1), (2, 3, 0, 0, 1, 0),
    (2, 3, 0, 0, 1, 1), (1, 0, 1, 0, 1, 0), (1, 0, 1, 0, 1, 1), (0, 0, 1, 0, 1, 0), (0, 0, 1, 0, 1, 1),
    (3, 1, 1, 0, 1, 0), (3, 1, 1, 0, 1, 1), (1, 1, 1, 0, 1, 0), (1, 1, 1, 0, 1, 1), (2, 0, 1, 0, 1, 0),
    (2, 0, 1, 0, 1, 1), (2, 2, 1, 0, 1, 0), (2, 2, 1, 0, 1, 1), (1, 3, 0, 0, 1, 0), (1, 3, 0, 0, 1, 1),
    (3, 2, 1, 0, 1, 0), (3, 2, 1, 0, 1, 1), (3, 3, 1, 0, 1, 0), (3, 3, 1, 0, 1, 1), (1, 3, 0, 1, 0, 0),
    (2, 0, 0, 3, 0, 0), (2, 1, 0, 3, 0, 0), (0, 1, 0, 2, 0, 0), (0, 2, 0, 2, 0, 0), (2, 3, 0, 3, 0, 0),
    (1, 3, 0, 1, 0, 1), (2, 0, 0, 3, 0, 1), (2, 1, 0, 3, 0, 1), (0, 1, 0, 2, 0, 1), (0, 2, 0, 2, 0, 1),
    (2, 3, 0, 3, 0, 1), (1, 3, 0, 1, 1, 0), (3, 2, 0, 2, 1, 0), (0, 1, 0, 2, 1, 0), (1, 0, 0, 2, 1, 0),
    (1, 3, 0, 1, 1, 1), (3, 2, 0, 2, 1, 1), (0, 1, 0, 2, 1, 1), (1, 0, 0, 2, 1, 1),
)
HOME = (
    (1, 0, 0, 3, 1, 0), (1, 0, 0, 3, 1, 1), (3, 3, -1, 4, 0, 0), (3, 3, -1, 4, 0, 1), (3, 0, 0, 3, 0, 0),
    (3, 0, 0, 3, 0, 1), (1, 1, -1, 4, 0, 0), (1, 1, -1, 4, 0, 1), (0, 2, 0, 1, 1, 0), (0, 2, 0, 1, 1, 1),
    (3, 2, 0, 1, 1, 0), (3, 2, 0, 1, 1, 1), (0, 0, -1, 4, 1, 0), (0, 0, -1, 4, 1, 1), (0, 1, 0, 3, 1, 0),
    (0, 1, 0, 3, 1, 1), (2, 3, -1, 3, 1, 0), (2, 3, -1, 3, 1, 1), (2, 1, 0, 1, 1, 0), (2, 1, 0, 1, 1, 1),
    (1, 0, 0, 1, 0, 0), (1, 0, 0, 1, 0, 1), (2, 3, 0, 1, 0, 0), (2, 3, 0, 1, 0, 1), (3, 1, 0, 2, 0, 0),
    (3, 1, 0, 2, 0, 1), (0, 0, -1, 4, 0, 0), (0, 0, -1, 4, 0, 1), (1, 0, 0, 1, 1, 0), (1, 0, 0, 1, 1, 1),
    (3, 1, 0, 2, 1, 0), (3, 1, 0, 2, 1, 1), (2, 2, -1, 4, 0, 0), (0, 1, 0, 3, 0, 0), (2, 2, -1, 4, 0, 1),
    (0, 1, 0, 3, 0, 1), (3, 2, 0, 1, 0, 0), (3, 2, 0, 1, 0, 1), (1, 1, -1, 4, 1, 0), (1, 1, -1, 4, 1, 1),
    (3, 2, 0, 4, 1, 0), (3, 2, 0, 4, 1, 1), (0, 2, -1, 2, 0, 0), (0, 2, -1, 2, 0, 1), (0, 2, 0, 1, 0, 0),
    (0, 2, 0, 1, 0, 1), (0, 2, -1, 2, 1, 0), (0, 2, -1, 2, 1, 1), (1, 0, 0, 3, 0, 0), (1, 0, 0, 3, 0, 1),
    (2, 3, -1, 3, 0, 0), (2, 3, -1, 3, 0, 1), (1, 3, -1, 2, 1, 0), (1, 3, -1, 2, 1, 1), (2, 0, 0, 2, 0, 0),
    (2, 0, 0, 2, 0, 1), (1, 3, -1, 2, 0, 0), (1, 3, -1, 2, 0, 1), (2, 2, -1, 4, 1, 0), (2, 2, -1, 4, 1, 1),
    (3, 1, 0, 3, 1, 0), (3, 1, 0, 3, 1, 1), (2, 0, 0, 2, 1, 0), (2, 0, 0, 2, 1, 1),
)
PASS_ON = (
    ((1, 1, 0, 0), (0, 2, 0, 0), (2, 3, 0, 0)), ((1, 1, 0, 1), (0, 2, 0, 1), (2, 3, 0, 1), (1, 1, 1, 0), (3, 2, 1, 0), (0, 2, 1, 0), (1, 2, 1, 0)), ((1, 1, 1, 1), (3, 2, 1, 1)), ((0, 2, 1, 1), (1, 2, 1, 1)), (),
)
ADD_UP = (
    (), ((0, 2, 1, 0), (1, 1, 1, 0), (2, 3, 1, 0)), ((0, 2, 1, 1), (1, 4, 1, 0), (2, 3, 1, 1)), ((0, 2, 0, 0), (1, 4, 1, 1), (2, 3, 0, 0), (3, 2, 0, 0), (0, 2, 0, 1)), ((1, 4, 0, 0), (1, 1, 1, 1), (2, 3, 0, 1), (3, 2, 0, 1), (1, 4, 0, 1)),
)
FIRST = ((4, 2, 3, 1), (1, 2, 4, 3), (2, 3, 4, 1), (2, 1, 4, 3))
SECOND = ((4, 1, 3, 2), (3, 2, 1, 4), (4, 1, 2, 3), (4, 3, 1, 2))
GROUP = 4
f32 = jnp.float32
bf16 = jnp.bfloat16


def dot(a, b, ca, cb):
    return lax.dot_general(a, b, (((ca,), (cb,)), ((), ())), preferred_element_type=f32)


def rope(n, cosines, sines, half):
    return n * cosines + pltpu.roll(n, half, 1) * sines


def rope_back(g, cosines, sines, half):
    return g * cosines + pltpu.roll(g * sines, half, 1)


def inverse_rms(u):
    return lax.rsqrt(jnp.mean(u * u, axis=-1, keepdims=True) + norm_epsilon)


def norm_rope_back(g, u, gain, cosines, sines, half):
    r = inverse_rms(u)
    w = rope_back(g, cosines, sines, half) * gain
    return r * (w - u * (r * r * jnp.mean(w * u, axis=-1, keepdims=True)))


def step_of(a, b, ahead):
    return GROUP * ahead + b - a


def out_of(place, d, w, i):
    return [(b, g) for a, b, g, *piece in OUT if (a, *piece) == (place, d, w, i)]


def home_of(place, d, w, i):
    ((b, g),) = [(b, g) for a, b, g, *piece in HOME if (a, *piece) == (place, d, w, i)]
    return b, g


def inbound(place):
    return [(a, e, g, w, i) for a, b, g, e, w, i in HOME if b == place]


def givers(place, d, w, i):
    return [
        (a, e, g) for a, e, g, *piece in inbound(place)
        if piece == [w, i] and e + step_of(a, place, g) == d
    ]


def partners(place, g):
    pairs = {edge[:3] for edge in OUT + HOME}
    pairs |= {(b, a, -h) for a, b, h in pairs}
    return sorted(b for a, b, h in pairs if (a, h) == (place, g) and (b, g) != (place, 0))


SLOTS = max(len(inbound(place)) for place in range(GROUP))


def kernel(
    n_ctx, n_tp, reach, per_kv, kv_count, head, tiles,
    tokens, rgrad, qw, kw, vw, ow, qgain_in, kgain_in, freq_in,
    out_ref, gout_ref,
    wqkv, wo, xg, gg, raw, cos_t, sin_t, q_s, do_s, dot_s, kv_own, halo, e_s, dp_s,
    l_s, ot_s, dqt_s, att, dkv, own_grad, gin, back, part, rs_in, acc, rope_in,
    local_sem, ag_send, ag_recv, f_send, f_recv, b_send, b_recv, rs_send, rs_recv,
):
    c = lax.axis_index("ctx")
    t = lax.axis_index("tp")
    s = lax.rem(c, reach)
    z = lax.div(c, reach)
    nz = n_ctx // reach
    local, width = xg.shape[1], xg.shape[2]
    rows = local * n_tp
    half = head // 2
    qc = kv_count * per_kv * head
    kc = kv_count * head
    qn = per_kv * rows

    barrier = pltpu.get_barrier_semaphore()
    for j in range(1, n_tp):
        pl.semaphore_signal(
            barrier, inc=1, device_id={"tp": lax.rem(t + j, n_tp)}, device_id_type=MESH
        )
    def here(k, early=False, later=False):
        on = s == k
        if early:
            on = on & (z > 0)
        if later:
            on = on & (z + 1 < nz)
        return on

    def pick(by_place):
        value = jnp.int32(by_place[0])
        for k in range(1, reach):
            value = jnp.where(s == k, jnp.int32(by_place[k]), value)
        return value

    for k in range(reach):
        for g in (-1, 0, 1):
            if partners(k, g):
                @pl.when(here(k, early=g < 0, later=g > 0))
                def _(k=k, g=g):
                    for b in partners(k, g):
                        pl.semaphore_signal(
                            barrier, inc=1, device_id={"ctx": c + step_of(k, b, g)},
                            device_id_type=MESH,
                        )

    def local_copy(i, src, dst):
        return pltpu.make_async_copy(src, dst, local_sem.at[i])

    loads = [
        local_copy(0, tokens, xg.at[0]),
        local_copy(1, qw, wqkv.at[:, :qc]),
        local_copy(2, rgrad, gg.at[0]),
        local_copy(3, ow, wo),
    ]
    kv_loads = [
        local_copy(4, kw, wqkv.at[:, qc : qc + kc]),
        local_copy(4, vw, wqkv.at[:, qc + kc : qc + 2 * kc]),
    ]
    table_loads = [local_copy(5, x, rope_in.at[i]) for i, x in enumerate((freq_in, kgain_in, qgain_in))]
    for load in table_loads + loads[:1] + kv_loads + loads[2:3] + loads[1:2] + loads[3:]:
        load.start()

    def to_ctx(src, dst, send, recv, target):
        return pltpu.make_async_remote_copy(
            src_ref=src, dst_ref=dst, send_sem=send, recv_sem=recv,
            device_id={"ctx": target}, device_id_type=MESH,
        )

    def to_tp(src, dst, send, recv, target):
        return pltpu.make_async_remote_copy(
            src_ref=src, dst_ref=dst, send_sem=send, recv_sem=recv,
            device_id={"tp": target}, device_id_type=MESH,
        )

    count = [[len(partners(k, g)) for k in range(reach)] for g in (-1, 0, 1)]
    none = jnp.int32(0)
    greeted = (
        n_tp - 1
        + jnp.where(z > 0, pick(count[0]), none)
        + pick(count[1])
        + jnp.where(z + 1 < nz, pick(count[2]), none)
    )
    def place(row):
        return lax.rem(t + lax.div(row, local), n_tp) * local + lax.rem(row, local)

    local_copy(5, rope_in, rope_in).wait()
    freq, kgain, qgain = rope_in.at[0], rope_in.at[1], rope_in.at[2]
    fold = rows // 2
    lane = lax.broadcasted_iota(jnp.int32, (fold, head), 1)
    low_lanes = lane < half
    row = lax.broadcasted_iota(jnp.int32, (fold, head), 0) + jnp.where(low_lanes, 0, fold)
    angles = (c * rows + place(row)).astype(f32) * freq[...]
    cosines, sines = jnp.cos(angles), jnp.sin(angles)
    cos_r, sin_r = pltpu.roll(cosines, half, 1), pltpu.roll(sines, half, 1)
    cos_t[:fold, :] = jnp.where(low_lanes, cosines, cos_r)
    cos_t[fold:, :] = jnp.where(low_lanes, cos_r, cosines)
    sin_t[:fold, :] = jnp.where(low_lanes, -sines, sin_r)
    sin_t[fold:, :] = jnp.where(low_lanes, -sin_r, sines)

    spans = (slice(0, local), slice(local, rows))
    chunks = [(w, i) for w in range(2) for i in range(2)]

    def key_values(w, x):
        span = spans[w]
        raw[span, qc : qc + 2 * kc] = x
        for m in range(kv_count):
            u = raw[span, qc + m * head : qc + (m + 1) * head]
            n = u * inverse_rms(u) * kgain[...]
            kv_own[0, m, span] = rope(n, cos_t[span, :], sin_t[span, :], half).astype(bf16)
            v0 = qc + kc + m * head
            kv_own[1, m, span] = raw[span, v0 : v0 + head].astype(bf16)

    def hop(a, b, g, d, w, i):
        span, e = spans[w], d + step_of(a, b, g)
        src = kv_own.at[i, :, span] if d == 0 else halo.at[d - 1, i, :, span]
        kind = 2 if g else int(d > a)
        return to_ctx(src, halo.at[e - 1, i, :, span], f_send.at[kind],
                      f_recv.at[e - 1, w, i], c + step_of(a, b, g))

    def arrived(d, w, i):
        span = spans[w]
        to_ctx(kv_own.at[i, :, span], halo.at[d - 1, i, :, span], f_send.at[2],
               f_recv.at[d - 1, w, i], c).wait_recv()

    settled = set()

    def settle(jobs):
        for k, d, w, i in jobs:
            if (k, d, w, i) in settled:
                continue
            settled.add((k, d, w, i))

            @pl.when(here(k, early=d > k))
            def _(k=k, d=d, w=w, i=i):
                arrived(d, w, i)
                for b, g in out_of(k, d, w, i):
                    hop(k, b, g, d, w, i).start()

    pl.semaphore_wait(barrier, greeted)

    cuts = (*range(0, width, 768), width)
    pieces = len(cuts) - 1

    def gather(w, j, n):
        dst = xg if w == 0 else gg
        cols = slice(cuts[n], cuts[n + 1]) if w == 0 else slice(None)
        return to_tp(dst.at[0, :, cols], dst.at[n_tp - j, :, cols], ag_send,
                     ag_recv.at[w * pieces + n, j - 1], lax.rem(t + j, n_tp))

    loads[0].wait()
    for n in range(pieces):
        for j in range(1, n_tp):
            gather(0, j, n).start()


    local_copy(4, wqkv.at[:, qc:], wqkv.at[:, qc:]).wait()
    key_values(0, dot(xg[0], wqkv[:, qc:], 1, 0))

    def send_own(w):
        for k in range(reach):
            for ahead in (1, 0):
                targets = [
                    (b, i) for a, b, g, d, v, i in OUT if (a, g, d, v) == (k, ahead, 0, w)
                ]
                if targets:
                    @pl.when(here(k, later=ahead > 0))
                    def _(k=k, ahead=ahead, targets=targets):
                        for b, i in targets:
                            hop(k, b, ahead, 0, w, i).start()

    send_own(0)
    loads[2].wait()
    for j in range(1, n_tp):
        gather(1, j, 0).start()
    projected = None
    for n in range(pieces):
        cols = slice(cuts[n], cuts[n + 1])
        for j in range(1, n_tp):
            gather(0, j, n).wait_recv()
        x = xg[1:, :, cols].reshape(rows - local, cuts[n + 1] - cuts[n])
        piece = dot(x, wqkv[cols, qc:], 1, 0)
        projected = piece if n == 0 else projected + piece
    key_values(1, projected)
    send_own(1)

    loads[1].wait()
    raw[:, :qc] = dot(xg[...].reshape(rows, width), wqkv[:, :qc], 1, 0)
    for h in range(kv_count * per_kv):
        m, g = h // per_kv, h % per_kv
        u = raw[:, h * head : (h + 1) * head]
        n = u * inverse_rms(u) * qgain[...]
        q_s[m, g * rows : (g + 1) * rows] = rope(n, cos_t[...], sin_t[...], half).astype(bf16)
    settle(PASS_ON[0])

    loads[3].wait()
    for j in range(1, n_tp):
        gather(1, j, 0).wait_recv()
    d_out = dot(gg[...].reshape(rows, width), wo[...], 1, 1).astype(bf16)
    for h in range(kv_count * per_kv):
        m, g = h // per_kv, h % per_kv
        piece = d_out[:, h * head : (h + 1) * head]
        do_s[m, g * rows : (g + 1) * rows] = piece
        dot_s[m, :, g * rows : (g + 1) * rows] = piece.astype(f32).T
    settle(PASS_ON[1])

    def kv(d, w, m):
        return kv_own[w, m] if isinstance(d, int) and d == 0 else halo[d - 1, w, m]

    def first_pass(d):
        for m in range(kv_count):
            key, value = kv(d, 0, m), kv(d, 1, m)
            e = jnp.exp(dot(key, q_s[m], 1, 1) * score_scale)
            key_row = place(lax.broadcasted_iota(jnp.int32, (rows, 1), 0))
            query_row = place(
                lax.rem(lax.broadcasted_iota(jnp.int32, (1, qn), 1), jnp.int32(rows))
            )
            if isinstance(d, int):
                keep = query_row >= key_row
            else:
                keep = query_row < key_row + jnp.where(d == reach, 0, rows)
            e = jnp.where(keep, e, f32(0.0))
            total = jnp.sum(e, axis=0, keepdims=True)
            low = e.astype(bf16)
            e_s[d, m] = low
            mixed = dot(value, low, 0, 0)
            dp_s[d, m] = dot(value, do_s[m], 1, 1) * score_scale
            if isinstance(d, int) and d == 0:
                l_s[m] = total
                ot_s[m] = mixed
            else:
                l_s[m] += total
                ot_s[m] += mixed

    first_pass(0)

    settle(PASS_ON[2])
    for step in range(reach):
        for k in range(reach):
            settle([(k, FIRST[k][step], w, i) for w, i in chunks])
        far = pick([order[step] for order in FIRST])

        @pl.when(c >= far)
        def _(far=far):
            first_pass(far)

        if step < 2:
            settle(PASS_ON[3 + step])

    inv, delta = [], []
    for m in range(kv_count):
        inv.append(1.0 / l_s[m])
        o_t = (ot_s[m] * inv[m]).astype(bf16).astype(f32)
        delta.append(jnp.sum(o_t * dot_s[m], axis=0, keepdims=True) * score_scale)
        for g in range(per_kv):
            h = m * per_kv + g
            att[:, h * head : (h + 1) * head] = o_t[:, g * rows : (g + 1) * rows].T.astype(bf16)
        dqt_s[m] = jnp.zeros_like(dqt_s[m])

    def second_pass(d, m):
        p = e_s[d, m].astype(f32) * inv[m]
        ds = (p * (dp_s[d, m] - delta[m])).astype(bf16)
        dk = dot(ds, q_s[m], 1, 0)
        dv = dot(p.astype(bf16), do_s[m], 1, 0)
        dqt_s[m] += dot(kv(d, 0, m), ds, 0, 0)
        return dk, dv

    def give(k, d, w, i):
        span = spans[w]
        b, g = home_of(k, d, w, i)
        n = inbound(b).index((k, d, g, w, i))
        return to_ctx(dkv.at[d - 1, i, :, span], gin.at[n, :, span],
                      b_send.at[int(d > k)], b_recv.at[n], c + step_of(k, b, g))

    def taken(k, giver, w, i):
        span = spans[w]
        n = inbound(k).index((*giver, w, i))
        to_ctx(dkv.at[0, i, :, span], gin.at[n, :, span], b_send.at[0], b_recv.at[n], c).wait_recv()
        return gin[n, :, span].astype(f32)

    def combine(jobs):
        for k, d, w, i in jobs:
            @pl.when(here(k, early=d > k))
            def _(k=k, d=d, w=w, i=i):
                span = spans[w]
                total = dkv[d - 1, i, :, span].astype(f32)
                for giver in givers(k, d, w, i):
                    total += taken(k, giver, w, i)
                dkv[d - 1, i, :, span] = total.astype(bf16)
                give(k, d, w, i).start()

    for step in range(reach):
        far = pick([order[step] for order in SECOND])

        @pl.when(c >= far)
        def _(step=step, far=far):
            for m in range(kv_count):
                dk, dv = second_pass(far, m)
                dkv[far - 1, 0, m] = dk.astype(bf16)
                dkv[far - 1, 1, m] = dv.astype(bf16)
            for k in range(reach):
                d = SECOND[k][step]
                leaves = [
                    (w, i) for a, _, _, e, w, i in HOME
                    if (a, e) == (k, d) and not givers(k, d, w, i)
                ]
                if leaves:
                    @pl.when(here(k))
                    def _(k=k, d=d, leaves=leaves):
                        for w, i in leaves:
                            give(k, d, w, i).start()

    for m in range(kv_count):
        dk, dv = second_pass(0, m)
        own_grad[0, m] = dk
        own_grad[1, m] = dv

    def rs_copy(w, j, n):
        cols = slice(*tiles[n])
        return to_tp(part.at[w, j, :, cols], rs_in.at[w, j - 1, :, cols], rs_send,
                     rs_recv.at[w + n if w == 2 else w, j - 1], lax.rem(t + j, n_tp))

    def product(lhs, n, first, last, by_row):
        cols = slice(*tiles[n])
        if by_row:
            return dot(lhs, wo[:, cols], 1, 0)
        return dot(lhs, wqkv[cols, first:last], 1, 1)

    def project(w, lhs, base, first, last, by_row):
        for n, (lo, hi) in enumerate(tiles):
            both = product(lhs, n, first, last, by_row)
            acc[w, :, lo:hi] = base[0, :, lo:hi].astype(f32) + both[:local]
            for j in range(1, n_tp):
                part[w, j, :, lo:hi] = both[j * local : (j + 1) * local].astype(bf16)

    def exchange(w):
        for j in range(1, n_tp):
            to_tp(part.at[w, j], rs_in.at[w, j - 1], rs_send, rs_recv.at[w, j - 1],
                  lax.rem(t + j, n_tp)).start()

    combine(ADD_UP[0])
    project(0, att[...], xg, 0, qc, True)
    combine(ADD_UP[1])
    for m in range(kv_count):
        for g in range(per_kv):
            h = m * per_kv + g
            grad = dqt_s[m, :, g * rows : (g + 1) * rows].T
            u = raw[:, h * head : (h + 1) * head]
            back[:, h * head : (h + 1) * head] = norm_rope_back(
                grad, u, qgain[...], cos_t[...], sin_t[...], half
            ).astype(bf16)
    combine(ADD_UP[2])
    exchange(0)
    project(1, back[:, :qc], gg, 0, qc, False)
    combine(ADD_UP[3])
    combine(ADD_UP[4])
    exchange(1)
    def landed(w):
        for j in range(1, n_tp):
            block = part.at[w, j]
            to_tp(block, rs_in.at[w, j - 1], rs_send, rs_recv.at[w, j - 1], t).wait_recv()
        return sum(rs_in[w, j - 1].astype(f32) for j in range(1, n_tp))

    out_ref[...] = (acc[0] + landed(0)).astype(bf16)
    acc[1] += landed(1)

    for w in (1, 0):
        span = spans[w]
        for i in range(2):
            for k in range(reach):
                for later in (False, True):
                    mine = [x for x in givers(k, 0, w, i) if bool(x[2]) == later]
                    if mine:
                        @pl.when(here(k, later=later))
                        def _(k=k, mine=mine, w=w, i=i, span=span):
                            for giver in mine:
                                own_grad[i, :, span] += taken(k, giver, w, i)

        for m in range(kv_count):
            k0 = qc + m * head
            u = raw[span, k0 : k0 + head]
            back[span, k0 : k0 + head] = norm_rope_back(
                own_grad[0, m, span], u, kgain[...], cos_t[span, :], sin_t[span, :], half
            ).astype(bf16)
            back[span, k0 + kc : k0 + kc + head] = own_grad[1, m, span].astype(bf16)

        for n, (lo, hi) in enumerate(tiles):
            piece = product(back[span, qc:], n, qc, qc + 2 * kc, False)
            if w == 0:
                acc[1, :, lo:hi] += piece
            else:
                for j in range(1, n_tp):
                    part[2, j, :, lo:hi] = piece[(j - 1) * local : j * local].astype(bf16)
                    rs_copy(2, j, n).start()
    for n, (lo, hi) in enumerate(tiles):
        total = acc[1, :, lo:hi]
        for j in range(1, n_tp):
            rs_copy(2, j, n).wait_recv()
            total += rs_in[2, j - 1, :, lo:hi].astype(f32)
        gout_ref[:, lo:hi] = total.astype(bf16)

    def sent(sem, ref):
        pltpu.make_async_copy(ref, ref, sem).wait()

    sent(ag_send, part.at[:2, 1:])
    sent(rs_send, part.at[:, 1:])

    def drain(sem, ref, pieces):
        for w, i in chunks:
            if pieces.count((w, i)):
                sent(sem, ref.at[: pieces.count((w, i)), i, :, spans[w]])

    for k in range(reach):
        for kind in range(3):
            gone = [(w, i) for a, _, g, e, w, i in OUT if a == k and kind == (2 if g else int(e > a))]
            back_gone = [(w, i) for a, _, _, e, w, i in HOME if a == k and kind == int(e > a)]
            if gone or back_gone:
                @pl.when(here(k, early=kind == 1, later=kind == 2))
                def _(kind=kind, gone=gone, back_gone=back_gone):
                    drain(f_send.at[kind], halo, gone)
                    if kind < 2:
                        drain(b_send.at[kind], dkv, back_gone)


def write(a, b, a_out, b_out, sems):
    rows = a.shape[0]
    step = rows // 8 if rows % 64 == 0 else rows
    for w, (x, y) in enumerate(((a, a_out), (b, b_out))):
        for i in range(0, rows, step):
            pltpu.make_async_copy(x.at[pl.ds(i, step)], y.at[pl.ds(i, step)], sems.at[w]).start()
    for w, x in enumerate((a, b)):
        pltpu.make_async_copy(x, x, sems.at[w]).wait()


def on_device(
    tokens, result_grad, query_weight, key_weight, value_weight, output_weight, query_gain, key_gain
):
    n_ctx = lax.axis_size("ctx")
    n_tp = lax.axis_size("tp")
    local, width = tokens.shape
    rows = local * n_tp
    head = query_gain.shape[0]
    kv_count = key_weight.shape[1] // head
    per_kv = query_weight.shape[1] // key_weight.shape[1]
    reach = WINDOW // rows
    assert reach == GROUP and n_ctx % reach == 0
    qc = kv_count * per_kv * head
    kc = kv_count * head
    qn = per_kv * rows
    tiles = tuple((lo, min(lo + 1024, width)) for lo in range(0, width, 1024))
    exponent = np.arange(head // 2, dtype=np.float32) * np.float32(2.0 / head)
    frequency = np.power(np.float32(rope_theta), -exponent)
    frequency = jnp.asarray(np.concatenate([frequency, frequency])[None, :])
    any_spec = pl.BlockSpec(memory_space=pl.ANY)
    vmem_spec = pl.BlockSpec(memory_space=pltpu.VMEM)
    block = (2, kv_count, rows, head)
    dma = pltpu.SemaphoreType.DMA
    out = pltpu.VMEM((local, width), bf16)
    layer_output, tokens_grad = pl.pallas_call(
        functools.partial(kernel, n_ctx, n_tp, reach, per_kv, kv_count, head, tiles),
        out_shape=(out, out),
        in_specs=[any_spec] * 9,
        out_specs=(vmem_spec, vmem_spec),
        scratch_shapes=[
            pltpu.VMEM((width, qc + 2 * kc), bf16),
            pltpu.VMEM((qc, width), bf16),
            pltpu.VMEM((n_tp, local, width), bf16),
            pltpu.VMEM((n_tp, local, width), bf16),
            pltpu.VMEM((rows, qc + 2 * kc), f32),
            pltpu.VMEM((rows, head), f32),
            pltpu.VMEM((rows, head), f32),
            pltpu.VMEM((kv_count, qn, head), bf16),
            pltpu.VMEM((kv_count, qn, head), bf16),
            pltpu.VMEM((kv_count, head, qn), f32),
            pltpu.VMEM(block, bf16),
            pltpu.VMEM((reach,) + block, bf16),
            pltpu.VMEM((reach + 1, kv_count, rows, qn), bf16),
            pltpu.VMEM((reach + 1, kv_count, rows, qn), f32),
            pltpu.VMEM((kv_count, 1, qn), f32),
            pltpu.VMEM((kv_count, head, qn), f32),
            pltpu.VMEM((kv_count, head, qn), f32),
            pltpu.VMEM((rows, qc), bf16),
            pltpu.VMEM((reach,) + block, bf16),
            pltpu.VMEM(block, f32),
            pltpu.VMEM((SLOTS, kv_count, rows, head), bf16),
            pltpu.VMEM((rows, qc + 2 * kc), bf16),
            pltpu.VMEM((3, n_tp, local, width), bf16),
            pltpu.VMEM((3, n_tp - 1, local, width), bf16),
            pltpu.VMEM((2, local, width), f32),
            pltpu.VMEM((3, 1, head), f32),
            dma((6,)),
            dma,
            dma((pl.cdiv(width, 768) + 1, n_tp - 1)),
            dma((3,)),
            dma((reach, 2, 2)),
            dma((2,)),
            dma((SLOTS,)),
            dma,
            dma((2 + len(tiles), n_tp - 1)),
        ],
        compiler_params=pltpu.CompilerParams(
            collective_id=0, has_side_effects=True, vmem_limit_bytes=56 * 1024 * 1024
        ),
    )(
        tokens, result_grad, query_weight, key_weight, value_weight, output_weight,
        query_gain[None, :], key_gain[None, :], frequency,
    )
    result = jax.ShapeDtypeStruct((local, width), bf16)
    return pl.pallas_call(
        write,
        out_shape=(result, result),
        in_specs=[vmem_spec] * 2,
        out_specs=(any_spec, any_spec),
        scratch_shapes=[dma((2,))],
        compiler_params=pltpu.CompilerParams(vmem_limit_bytes=2 * 1024 * 1024),
    )(layer_output, tokens_grad)


def solution(mesh):
    in_specs = (
        P(("ctx", "tp"), None),
        P(("ctx", "tp"), None),
        P(None, "tp"),
        P(None, "tp"),
        P(None, "tp"),
        P("tp", None),
        P(),
        P(),
    )
    out_specs = (P(("ctx", "tp"), None), P(("ctx", "tp"), None))
    return jax.shard_map(
        on_device, mesh=mesh, in_specs=in_specs, out_specs=out_specs, check_vma=False
    )
```

```python
import functools

import jax
import jax.numpy as jnp
import numpy as np
from jax import lax
from jax.experimental import pallas as pl
from jax.experimental.pallas import tpu as pltpu
from jax.sharding import PartitionSpec as P

WINDOW = 1024
norm_epsilon = 1e-06
score_scale = 168.0 ** (-0.5)
rope_theta = 10000.0
MESH = pl.DeviceIdType.MESH
OUT = (
    (0, 0, 1, 0, 0, 0), (0, 0, 1, 0, 0, 1), (1, 3, 0, 0, 0, 0), (1, 3, 0, 0, 0, 1), (2, 3, 0, 0, 0, 0),
    (2, 3, 0, 0, 0, 1), (1, 1, 1, 0, 0, 0), (1, 1, 1, 0, 0, 1), (0, 2, 0, 0, 0, 0), (0, 2, 0, 0, 0, 1),
    (3, 2, 1, 0, 0, 0), (3, 2, 1, 0, 0, 1), (1, 2, 0, 0, 0, 0), (1, 2, 0, 0, 0, 1), (1, 0, 1, 0, 0, 0),
    (1, 0, 1, 0, 0, 1), (0, 1, 0, 0, 0, 0), (0, 1, 0, 0, 0, 1), (2, 0, 1, 0, 0, 0), (2, 0, 1, 0, 0, 1),
    (0, 2, 0, 0, 1, 0), (0, 2, 0, 0, 1, 1), (0, 1, 0, 0, 1, 0), (0, 1, 0, 0, 1, 1), (2, 3, 0, 0, 1, 0),
    (2, 3, 0, 0, 1, 1), (1, 0, 1, 0, 1, 0), (1, 0, 1, 0, 1, 1), (0, 0, 1, 0, 1, 0), (0, 0, 1, 0, 1, 1),
    (3, 1, 1, 0, 1, 0), (3, 1, 1, 0, 1, 1), (1, 1, 1, 0, 1, 0), (1, 1, 1, 0, 1, 1), (2, 0, 1, 0, 1, 0),
    (2, 0, 1, 0, 1, 1), (2, 2, 1, 0, 1, 0), (2, 2, 1, 0, 1, 1), (1, 3, 0, 0, 1, 0), (1, 3, 0, 0, 1, 1),
    (3, 2, 1, 0, 1, 0), (3, 2, 1, 0, 1, 1), (3, 3, 1, 0, 1, 0), (3, 3, 1, 0, 1, 1), (1, 3, 0, 1, 0, 0),
    (2, 0, 0, 3, 0, 0), (2, 1, 0, 3, 0, 0), (0, 1, 0, 2, 0, 0), (0, 2, 0, 2, 0, 0), (2, 3, 0, 3, 0, 0),
    (1, 3, 0, 1, 0, 1), (2, 0, 0, 3, 0, 1), (2, 1, 0, 3, 0, 1), (0, 1, 0, 2, 0, 1), (0, 2, 0, 2, 0, 1),
    (2, 3, 0, 3, 0, 1), (1, 3, 0, 1, 1, 0), (3, 2, 0, 2, 1, 0), (0, 1, 0, 2, 1, 0), (1, 0, 0, 2, 1, 0),
    (1, 3, 0, 1, 1, 1), (3, 2, 0, 2, 1, 1), (0, 1, 0, 2, 1, 1), (1, 0, 0, 2, 1, 1),
)
HOME = (
    (1, 0, 0, 3, 1, 0), (1, 0, 0, 3, 1, 1), (3, 3, -1, 4, 0, 0), (3, 3, -1, 4, 0, 1), (3, 0, 0, 3, 0, 0),
    (3, 0, 0, 3, 0, 1), (1, 1, -1, 4, 0, 0), (1, 1, -1, 4, 0, 1), (0, 2, 0, 1, 1, 0), (0, 2, 0, 1, 1, 1),
    (3, 2, 0, 1, 1, 0), (3, 2, 0, 1, 1, 1), (0, 0, -1, 4, 1, 0), (0, 0, -1, 4, 1, 1), (0, 1, 0, 3, 1, 0),
    (0, 1, 0, 3, 1, 1), (2, 3, -1, 3, 1, 0), (2, 3, -1, 3, 1, 1), (2, 1, 0, 1, 1, 0), (2, 1, 0, 1, 1, 1),
    (1, 0, 0, 1, 0, 0), (1, 0, 0, 1, 0, 1), (2, 3, 0, 1, 0, 0), (2, 3, 0, 1, 0, 1), (3, 1, 0, 2, 0, 0),
    (3, 1, 0, 2, 0, 1), (0, 0, -1, 4, 0, 0), (0, 0, -1, 4, 0, 1), (1, 0, 0, 1, 1, 0), (1, 0, 0, 1, 1, 1),
    (3, 1, 0, 2, 1, 0), (3, 1, 0, 2, 1, 1), (2, 2, -1, 4, 0, 0), (0, 1, 0, 3, 0, 0), (2, 2, -1, 4, 0, 1),
    (0, 1, 0, 3, 0, 1), (3, 2, 0, 1, 0, 0), (3, 2, 0, 1, 0, 1), (1, 1, -1, 4, 1, 0), (1, 1, -1, 4, 1, 1),
    (3, 2, 0, 4, 1, 0), (3, 2, 0, 4, 1, 1), (0, 2, -1, 2, 0, 0), (0, 2, -1, 2, 0, 1), (0, 2, 0, 1, 0, 0),
    (0, 2, 0, 1, 0, 1), (0, 2, -1, 2, 1, 0), (0, 2, -1, 2, 1, 1), (1, 0, 0, 3, 0, 0), (1, 0, 0, 3, 0, 1),
    (2, 3, -1, 3, 0, 0), (2, 3, -1, 3, 0, 1), (1, 3, -1, 2, 1, 0), (1, 3, -1, 2, 1, 1), (2, 0, 0, 2, 0, 0),
    (2, 0, 0, 2, 0, 1), (1, 3, -1, 2, 0, 0), (1, 3, -1, 2, 0, 1), (2, 2, -1, 4, 1, 0), (2, 2, -1, 4, 1, 1),
    (3, 1, 0, 3, 1, 0), (3, 1, 0, 3, 1, 1), (2, 0, 0, 2, 1, 0), (2, 0, 0, 2, 1, 1),
)
PASS_ON = (
    ((1, 1, 0, 0), (0, 2, 0, 0), (2, 3, 0, 0)), ((1, 1, 0, 1), (0, 2, 0, 1), (2, 3, 0, 1), (1, 1, 1, 0), (3, 2, 1, 0), (0, 2, 1, 0), (1, 2, 1, 0)), ((1, 1, 1, 1), (3, 2, 1, 1)), ((0, 2, 1, 1), (1, 2, 1, 1)), (),
)
ADD_UP = (
    (), ((0, 2, 1, 0), (1, 1, 1, 0), (2, 3, 1, 0)), ((0, 2, 1, 1), (1, 4, 1, 0), (2, 3, 1, 1)), ((0, 2, 0, 0), (1, 4, 1, 1), (2, 3, 0, 0), (3, 2, 0, 0), (0, 2, 0, 1)), ((1, 4, 0, 0), (1, 1, 1, 1), (2, 3, 0, 1), (3, 2, 0, 1), (1, 4, 0, 1)),
)
FIRST = ((4, 2, 3, 1), (1, 2, 4, 3), (2, 3, 4, 1), (2, 1, 4, 3))
SECOND = ((4, 1, 3, 2), (3, 2, 1, 4), (4, 1, 2, 3), (4, 3, 1, 2))
GROUP = 4
f32 = jnp.float32
bf16 = jnp.bfloat16


def dot(a, b, ca, cb):
    return lax.dot_general(a, b, (((ca,), (cb,)), ((), ())), preferred_element_type=f32)


def rope(n, cosines, sines, half):
    return n * cosines + pltpu.roll(n, half, 1) * sines


def rope_back(g, cosines, sines, half):
    return g * cosines + pltpu.roll(g * sines, half, 1)


def inverse_rms(u):
    return lax.rsqrt(jnp.mean(u * u, axis=-1, keepdims=True) + norm_epsilon)


def norm_rope_back(g, u, gain, cosines, sines, half):
    r = inverse_rms(u)
    w = rope_back(g, cosines, sines, half) * gain
    return r * (w - u * (r * r * jnp.mean(w * u, axis=-1, keepdims=True)))


def step_of(a, b, ahead):
    return GROUP * ahead + b - a


def out_of(place, d, w, i):
    return [(b, g) for a, b, g, *piece in OUT if (a, *piece) == (place, d, w, i)]


def home_of(place, d, w, i):
    ((b, g),) = [(b, g) for a, b, g, *piece in HOME if (a, *piece) == (place, d, w, i)]
    return b, g


def inbound(place):
    return [(a, e, g, w, i) for a, b, g, e, w, i in HOME if b == place]


def givers(place, d, w, i):
    return [
        (a, e, g) for a, e, g, *piece in inbound(place)
        if piece == [w, i] and e + step_of(a, place, g) == d
    ]


def partners(place, g):
    pairs = {edge[:3] for edge in OUT + HOME}
    pairs |= {(b, a, -h) for a, b, h in pairs}
    return sorted(b for a, b, h in pairs if (a, h) == (place, g) and (b, g) != (place, 0))


SLOTS = max(len(inbound(place)) for place in range(GROUP))


def kernel(
    n_ctx, n_tp, reach, per_kv, kv_count, head, tiles,
    tokens, rgrad, qw, kw, vw, ow, qgain_in, kgain_in, freq_in,
    out_ref, gout_ref,
    wqkv, wo, xg, gg, raw, cos_t, sin_t, q_s, do_s, dot_s, kv_own, halo, e_s, dp_s,
    l_s, ot_s, dqt_s, att, dkv, own_grad, gin, back, part, rs_in, acc, rope_in,
    local_sem, ag_send, ag_recv, f_send, f_recv, b_send, b_recv, rs_send, rs_recv,
):
    c = lax.axis_index("ctx")
    t = lax.axis_index("tp")
    s = lax.rem(c, reach)
    z = lax.div(c, reach)
    nz = n_ctx // reach
    local, width = xg.shape[1], xg.shape[2]
    rows = local * n_tp
    half = head // 2
    qc = kv_count * per_kv * head
    kc = kv_count * head
    qn = per_kv * rows

    barrier = pltpu.get_barrier_semaphore()
    for j in range(1, n_tp):
        pl.semaphore_signal(
            barrier, inc=1, device_id={"tp": lax.rem(t + j, n_tp)}, device_id_type=MESH
        )
    def here(k, early=False, later=False):
        on = s == k
        if early:
            on = on & (z > 0)
        if later:
            on = on & (z + 1 < nz)
        return on

    def pick(by_place):
        value = jnp.int32(by_place[0])
        for k in range(1, reach):
            value = jnp.where(s == k, jnp.int32(by_place[k]), value)
        return value

    for k in range(reach):
        for g in (-1, 0, 1):
            if partners(k, g):
                @pl.when(here(k, early=g < 0, later=g > 0))
                def _(k=k, g=g):
                    for b in partners(k, g):
                        pl.semaphore_signal(
                            barrier, inc=1, device_id={"ctx": c + step_of(k, b, g)},
                            device_id_type=MESH,
                        )

    def local_copy(i, src, dst):
        return pltpu.make_async_copy(src, dst, local_sem.at[i])

    loads = [
        local_copy(0, tokens, xg.at[0]),
        local_copy(1, qw, wqkv.at[:, :qc]),
        local_copy(2, rgrad, gg.at[0]),
        local_copy(3, ow, wo),
    ]
    kv_loads = [
        local_copy(4, kw, wqkv.at[:, qc : qc + kc]),
        local_copy(4, vw, wqkv.at[:, qc + kc : qc + 2 * kc]),
    ]
    table_loads = [local_copy(5, x, rope_in.at[i]) for i, x in enumerate((freq_in, kgain_in, qgain_in))]
    for load in table_loads + loads[:1] + kv_loads + loads[2:3] + loads[1:2] + loads[3:]:
        load.start()

    def to_ctx(src, dst, send, recv, target):
        return pltpu.make_async_remote_copy(
            src_ref=src, dst_ref=dst, send_sem=send, recv_sem=recv,
            device_id={"ctx": target}, device_id_type=MESH,
        )

    def to_tp(src, dst, send, recv, target):
        return pltpu.make_async_remote_copy(
            src_ref=src, dst_ref=dst, send_sem=send, recv_sem=recv,
            device_id={"tp": target}, device_id_type=MESH,
        )

    count = [[len(partners(k, g)) for k in range(reach)] for g in (-1, 0, 1)]
    none = jnp.int32(0)
    greeted = (
        n_tp - 1
        + jnp.where(z > 0, pick(count[0]), none)
        + pick(count[1])
        + jnp.where(z + 1 < nz, pick(count[2]), none)
    )
    def place(row):
        return lax.rem(t + lax.div(row, local), n_tp) * local + lax.rem(row, local)

    local_copy(5, rope_in, rope_in).wait()
    freq, kgain, qgain = rope_in.at[0], rope_in.at[1], rope_in.at[2]
    fold = rows // 2
    lane = lax.broadcasted_iota(jnp.int32, (fold, head), 1)
    low_lanes = lane < half
    row = lax.broadcasted_iota(jnp.int32, (fold, head), 0) + jnp.where(low_lanes, 0, fold)
    angles = (c * rows + place(row)).astype(f32) * freq[...]
    cosines, sines = jnp.cos(angles), jnp.sin(angles)
    cos_r, sin_r = pltpu.roll(cosines, half, 1), pltpu.roll(sines, half, 1)
    cos_t[:fold, :] = jnp.where(low_lanes, cosines, cos_r)
    cos_t[fold:, :] = jnp.where(low_lanes, cos_r, cosines)
    sin_t[:fold, :] = jnp.where(low_lanes, -sines, sin_r)
    sin_t[fold:, :] = jnp.where(low_lanes, -sin_r, sines)

    spans = (slice(0, local), slice(local, rows))
    chunks = [(w, i) for w in range(2) for i in range(2)]

    def key_values(w, x):
        span = spans[w]
        raw[span, qc : qc + 2 * kc] = x
        for m in range(kv_count):
            u = raw[span, qc + m * head : qc + (m + 1) * head]
            n = u * inverse_rms(u) * kgain[...]
            kv_own[0, m, span] = rope(n, cos_t[span, :], sin_t[span, :], half).astype(bf16)
            v0 = qc + kc + m * head
            kv_own[1, m, span] = raw[span, v0 : v0 + head].astype(bf16)

    def hop(a, b, g, d, w, i):
        span, e = spans[w], d + step_of(a, b, g)
        src = kv_own.at[i, :, span] if d == 0 else halo.at[d - 1, i, :, span]
        kind = 2 if g else int(d > a)
        return to_ctx(src, halo.at[e - 1, i, :, span], f_send.at[kind],
                      f_recv.at[e - 1, w, i], c + step_of(a, b, g))

    def arrived(d, w, i):
        span = spans[w]
        to_ctx(kv_own.at[i, :, span], halo.at[d - 1, i, :, span], f_send.at[2],
               f_recv.at[d - 1, w, i], c).wait_recv()

    settled = set()

    def settle(jobs):
        for k, d, w, i in jobs:
            if (k, d, w, i) in settled:
                continue
            settled.add((k, d, w, i))

            @pl.when(here(k, early=d > k))
            def _(k=k, d=d, w=w, i=i):
                arrived(d, w, i)
                for b, g in out_of(k, d, w, i):
                    hop(k, b, g, d, w, i).start()

    pl.semaphore_wait(barrier, greeted)

    cuts = (*range(0, width, 768), width)
    pieces = len(cuts) - 1

    def gather(w, j, n):
        dst = xg if w == 0 else gg
        cols = slice(cuts[n], cuts[n + 1]) if w == 0 else slice(None)
        return to_tp(dst.at[0, :, cols], dst.at[n_tp - j, :, cols], ag_send,
                     ag_recv.at[w * pieces + n, j - 1], lax.rem(t + j, n_tp))

    loads[0].wait()
    for n in range(pieces):
        for j in range(1, n_tp):
            gather(0, j, n).start()


    local_copy(4, wqkv.at[:, qc:], wqkv.at[:, qc:]).wait()
    key_values(0, dot(xg[0], wqkv[:, qc:], 1, 0))

    def send_own(w):
        for k in range(reach):
            for ahead in (1, 0):
                targets = [
                    (b, i) for a, b, g, d, v, i in OUT if (a, g, d, v) == (k, ahead, 0, w)
                ]
                if targets:
                    @pl.when(here(k, later=ahead > 0))
                    def _(k=k, ahead=ahead, targets=targets):
                        for b, i in targets:
                            hop(k, b, ahead, 0, w, i).start()

    send_own(0)
    loads[2].wait()
    for j in range(1, n_tp):
        gather(1, j, 0).start()
    projected = None
    for n in range(pieces):
        cols = slice(cuts[n], cuts[n + 1])
        for j in range(1, n_tp):
            gather(0, j, n).wait_recv()
        x = xg[1:, :, cols].reshape(rows - local, cuts[n + 1] - cuts[n])
        piece = dot(x, wqkv[cols, qc:], 1, 0)
        projected = piece if n == 0 else projected + piece
    key_values(1, projected)
    send_own(1)

    loads[1].wait()
    raw[:, :qc] = dot(xg[...].reshape(rows, width), wqkv[:, :qc], 1, 0)
    for h in range(kv_count * per_kv):
        m, g = h // per_kv, h % per_kv
        u = raw[:, h * head : (h + 1) * head]
        n = u * inverse_rms(u) * qgain[...]
        q_s[m, g * rows : (g + 1) * rows] = rope(n, cos_t[...], sin_t[...], half).astype(bf16)
    settle(PASS_ON[0])

    loads[3].wait()
    for j in range(1, n_tp):
        gather(1, j, 0).wait_recv()
    d_out = dot(gg[...].reshape(rows, width), wo[...], 1, 1).astype(bf16)
    for h in range(kv_count * per_kv):
        m, g = h // per_kv, h % per_kv
        piece = d_out[:, h * head : (h + 1) * head]
        do_s[m, g * rows : (g + 1) * rows] = piece
        dot_s[m, :, g * rows : (g + 1) * rows] = piece.astype(f32).T
    settle(PASS_ON[1])

    def kv(d, w, m):
        return kv_own[w, m] if isinstance(d, int) and d == 0 else halo[d - 1, w, m]

    def first_pass(d):
        for m in range(kv_count):
            key, value = kv(d, 0, m), kv(d, 1, m)
            e = jnp.exp(dot(key, q_s[m], 1, 1) * score_scale)
            key_row = place(lax.broadcasted_iota(jnp.int32, (rows, 1), 0))
            query_row = place(
                lax.rem(lax.broadcasted_iota(jnp.int32, (1, qn), 1), jnp.int32(rows))
            )
            if isinstance(d, int):
                keep = query_row >= key_row
            else:
                keep = query_row < key_row + jnp.where(d == reach, 0, rows)
            e = jnp.where(keep, e, f32(0.0))
            total = jnp.sum(e, axis=0, keepdims=True)
            low = e.astype(bf16)
            e_s[d, m] = low
            mixed = dot(value, low, 0, 0)
            dp_s[d, m] = dot(value, do_s[m], 1, 1) * score_scale
            if isinstance(d, int) and d == 0:
                l_s[m] = total
                ot_s[m] = mixed
            else:
                l_s[m] += total
                ot_s[m] += mixed

    first_pass(0)

    settle(PASS_ON[2])
    for step in range(reach):
        for k in range(reach):
            settle([(k, FIRST[k][step], w, i) for w, i in chunks])
        far = pick([order[step] for order in FIRST])

        @pl.when(c >= far)
        def _(far=far):
            first_pass(far)

        if step < 2:
            settle(PASS_ON[3 + step])

    inv, delta = [], []
    for m in range(kv_count):
        inv.append(1.0 / l_s[m])
        o_t = (ot_s[m] * inv[m]).astype(bf16).astype(f32)
        delta.append(jnp.sum(o_t * dot_s[m], axis=0, keepdims=True) * score_scale)
        for g in range(per_kv):
            h = m * per_kv + g
            att[:, h * head : (h + 1) * head] = o_t[:, g * rows : (g + 1) * rows].T.astype(bf16)
        dqt_s[m] = jnp.zeros_like(dqt_s[m])

    def second_pass(d, m):
        p = e_s[d, m].astype(f32) * inv[m]
        ds = (p * (dp_s[d, m] - delta[m])).astype(bf16)
        dk = dot(ds, q_s[m], 1, 0)
        dv = dot(p.astype(bf16), do_s[m], 1, 0)
        dqt_s[m] += dot(kv(d, 0, m), ds, 0, 0)
        return dk, dv

    def give(k, d, w, i):
        span = spans[w]
        b, g = home_of(k, d, w, i)
        n = inbound(b).index((k, d, g, w, i))
        return to_ctx(dkv.at[d - 1, i, :, span], gin.at[n, :, span],
                      b_send.at[int(d > k)], b_recv.at[n], c + step_of(k, b, g))

    def taken(k, giver, w, i):
        span = spans[w]
        n = inbound(k).index((*giver, w, i))
        to_ctx(dkv.at[0, i, :, span], gin.at[n, :, span], b_send.at[0], b_recv.at[n], c).wait_recv()
        return gin[n, :, span].astype(f32)

    def combine(jobs):
        for k, d, w, i in jobs:
            @pl.when(here(k, early=d > k))
            def _(k=k, d=d, w=w, i=i):
                span = spans[w]
                total = dkv[d - 1, i, :, span].astype(f32)
                for giver in givers(k, d, w, i):
                    total += taken(k, giver, w, i)
                dkv[d - 1, i, :, span] = total.astype(bf16)
                give(k, d, w, i).start()

    for step in range(reach):
        far = pick([order[step] for order in SECOND])

        @pl.when(c >= far)
        def _(step=step, far=far):
            for m in range(kv_count):
                dk, dv = second_pass(far, m)
                dkv[far - 1, 0, m] = dk.astype(bf16)
                dkv[far - 1, 1, m] = dv.astype(bf16)
            for k in range(reach):
                d = SECOND[k][step]
                leaves = [
                    (w, i) for a, _, _, e, w, i in HOME
                    if (a, e) == (k, d) and not givers(k, d, w, i)
                ]
                if leaves:
                    @pl.when(here(k))
                    def _(k=k, d=d, leaves=leaves):
                        for w, i in leaves:
                            give(k, d, w, i).start()

    for m in range(kv_count):
        dk, dv = second_pass(0, m)
        own_grad[0, m] = dk
        own_grad[1, m] = dv

    def rs_copy(w, j, n):
        cols = slice(*tiles[n])
        return to_tp(part.at[w, j, :, cols], rs_in.at[w, j - 1, :, cols], rs_send,
                     rs_recv.at[w + n if w == 2 else w, j - 1], lax.rem(t + j, n_tp))

    def product(lhs, n, first, last, by_row):
        cols = slice(*tiles[n])
        if by_row:
            return dot(lhs, wo[:, cols], 1, 0)
        return dot(lhs, wqkv[cols, first:last], 1, 1)

    def project(w, lhs, base, first, last, by_row):
        for n, (lo, hi) in enumerate(tiles):
            both = product(lhs, n, first, last, by_row)
            acc[w, :, lo:hi] = base[0, :, lo:hi].astype(f32) + both[:local]
            for j in range(1, n_tp):
                part[w, j, :, lo:hi] = both[j * local : (j + 1) * local].astype(bf16)

    def exchange(w):
        for j in range(1, n_tp):
            to_tp(part.at[w, j], rs_in.at[w, j - 1], rs_send, rs_recv.at[w, j - 1],
                  lax.rem(t + j, n_tp)).start()

    combine(ADD_UP[0])
    project(0, att[...], xg, 0, qc, True)
    combine(ADD_UP[1])
    for m in range(kv_count):
        for g in range(per_kv):
            h = m * per_kv + g
            grad = dqt_s[m, :, g * rows : (g + 1) * rows].T
            u = raw[:, h * head : (h + 1) * head]
            back[:, h * head : (h + 1) * head] = norm_rope_back(
                grad, u, qgain[...], cos_t[...], sin_t[...], half
            ).astype(bf16)
    combine(ADD_UP[2])
    exchange(0)
    project(1, back[:, :qc], gg, 0, qc, False)
    combine(ADD_UP[3])
    combine(ADD_UP[4])
    exchange(1)
    def landed(w):
        for j in range(1, n_tp):
            block = part.at[w, j]
            to_tp(block, rs_in.at[w, j - 1], rs_send, rs_recv.at[w, j - 1], t).wait_recv()
        return sum(rs_in[w, j - 1].astype(f32) for j in range(1, n_tp))

    out_ref[...] = (acc[0] + landed(0)).astype(bf16)
    acc[1] += landed(1)

    for w in (1, 0):
        span = spans[w]
        for i in range(2):
            for k in range(reach):
                for later in (False, True):
                    mine = [x for x in givers(k, 0, w, i) if bool(x[2]) == later]
                    if mine:
                        @pl.when(here(k, later=later))
                        def _(k=k, mine=mine, w=w, i=i, span=span):
                            for giver in mine:
                                own_grad[i, :, span] += taken(k, giver, w, i)

        for m in range(kv_count):
            k0 = qc + m * head
            u = raw[span, k0 : k0 + head]
            back[span, k0 : k0 + head] = norm_rope_back(
                own_grad[0, m, span], u, kgain[...], cos_t[span, :], sin_t[span, :], half
            ).astype(bf16)
            back[span, k0 + kc : k0 + kc + head] = own_grad[1, m, span].astype(bf16)

        for n, (lo, hi) in enumerate(tiles):
            piece = product(back[span, qc:], n, qc, qc + 2 * kc, False)
            if w == 0:
                total = acc[1, :, lo:hi] + piece
                for j in range(1, n_tp):
                    rs_copy(2, j, n).wait_recv()
                    total += rs_in[2, j - 1, :, lo:hi].astype(f32)
                gout_ref[:, lo:hi] = total.astype(bf16)
            else:
                for j in range(1, n_tp):
                    part[2, j, :, lo:hi] = piece[(j - 1) * local : j * local].astype(bf16)
                    rs_copy(2, j, n).start()
    def sent(sem, ref):
        pltpu.make_async_copy(ref, ref, sem).wait()

    sent(ag_send, part.at[:2, 1:])
    sent(rs_send, part.at[:, 1:])

    def drain(sem, ref, pieces):
        for w, i in chunks:
            if pieces.count((w, i)):
                sent(sem, ref.at[: pieces.count((w, i)), i, :, spans[w]])

    for k in range(reach):
        for kind in range(3):
            gone = [(w, i) for a, _, g, e, w, i in OUT if a == k and kind == (2 if g else int(e > a))]
            back_gone = [(w, i) for a, _, _, e, w, i in HOME if a == k and kind == int(e > a)]
            if gone or back_gone:
                @pl.when(here(k, early=kind == 1, later=kind == 2))
                def _(kind=kind, gone=gone, back_gone=back_gone):
                    drain(f_send.at[kind], halo, gone)
                    if kind < 2:
                        drain(b_send.at[kind], dkv, back_gone)


def write(a, b, a_out, b_out, sems):
    rows = a.shape[0]
    step = rows // 8 if rows % 64 == 0 else rows
    for w, (x, y) in enumerate(((a, a_out), (b, b_out))):
        for i in range(0, rows, step):
            pltpu.make_async_copy(x.at[pl.ds(i, step)], y.at[pl.ds(i, step)], sems.at[w]).start()
    for w, x in enumerate((a, b)):
        pltpu.make_async_copy(x, x, sems.at[w]).wait()


def on_device(
    tokens, result_grad, query_weight, key_weight, value_weight, output_weight, query_gain, key_gain
):
    n_ctx = lax.axis_size("ctx")
    n_tp = lax.axis_size("tp")
    local, width = tokens.shape
    rows = local * n_tp
    head = query_gain.shape[0]
    kv_count = key_weight.shape[1] // head
    per_kv = query_weight.shape[1] // key_weight.shape[1]
    reach = WINDOW // rows
    assert reach == GROUP and n_ctx % reach == 0
    qc = kv_count * per_kv * head
    kc = kv_count * head
    qn = per_kv * rows
    tiles = tuple((lo, min(lo + 1024, width)) for lo in range(0, width, 1024))
    exponent = np.arange(head // 2, dtype=np.float32) * np.float32(2.0 / head)
    frequency = np.power(np.float32(rope_theta), -exponent)
    frequency = jnp.asarray(np.concatenate([frequency, frequency])[None, :])
    any_spec = pl.BlockSpec(memory_space=pl.ANY)
    vmem_spec = pl.BlockSpec(memory_space=pltpu.VMEM)
    block = (2, kv_count, rows, head)
    dma = pltpu.SemaphoreType.DMA
    out = pltpu.VMEM((local, width), bf16)
    layer_output, tokens_grad = pl.pallas_call(
        functools.partial(kernel, n_ctx, n_tp, reach, per_kv, kv_count, head, tiles),
        out_shape=(out, out),
        in_specs=[any_spec] * 9,
        out_specs=(vmem_spec, vmem_spec),
        scratch_shapes=[
            pltpu.VMEM((width, qc + 2 * kc), bf16),
            pltpu.VMEM((qc, width), bf16),
            pltpu.VMEM((n_tp, local, width), bf16),
            pltpu.VMEM((n_tp, local, width), bf16),
            pltpu.VMEM((rows, qc + 2 * kc), f32),
            pltpu.VMEM((rows, head), f32),
            pltpu.VMEM((rows, head), f32),
            pltpu.VMEM((kv_count, qn, head), bf16),
            pltpu.VMEM((kv_count, qn, head), bf16),
            pltpu.VMEM((kv_count, head, qn), f32),
            pltpu.VMEM(block, bf16),
            pltpu.VMEM((reach,) + block, bf16),
            pltpu.VMEM((reach + 1, kv_count, rows, qn), bf16),
            pltpu.VMEM((reach + 1, kv_count, rows, qn), f32),
            pltpu.VMEM((kv_count, 1, qn), f32),
            pltpu.VMEM((kv_count, head, qn), f32),
            pltpu.VMEM((kv_count, head, qn), f32),
            pltpu.VMEM((rows, qc), bf16),
            pltpu.VMEM((reach,) + block, bf16),
            pltpu.VMEM(block, f32),
            pltpu.VMEM((SLOTS, kv_count, rows, head), bf16),
            pltpu.VMEM((rows, qc + 2 * kc), bf16),
            pltpu.VMEM((3, n_tp, local, width), bf16),
            pltpu.VMEM((3, n_tp - 1, local, width), bf16),
            pltpu.VMEM((2, local, width), f32),
            pltpu.VMEM((3, 1, head), f32),
            dma((6,)),
            dma,
            dma((pl.cdiv(width, 768) + 1, n_tp - 1)),
            dma((3,)),
            dma((reach, 2, 2)),
            dma((2,)),
            dma((SLOTS,)),
            dma,
            dma((2 + len(tiles), n_tp - 1)),
        ],
        compiler_params=pltpu.CompilerParams(
            collective_id=0, has_side_effects=True, vmem_limit_bytes=56 * 1024 * 1024
        ),
    )(
        tokens, result_grad, query_weight, key_weight, value_weight, output_weight,
        query_gain[None, :], key_gain[None, :], frequency,
    )
    result = jax.ShapeDtypeStruct((local, width), bf16)
    return pl.pallas_call(
        write,
        out_shape=(result, result),
        in_specs=[vmem_spec] * 2,
        out_specs=(any_spec, any_spec),
        scratch_shapes=[dma((2,))],
        compiler_params=pltpu.CompilerParams(vmem_limit_bytes=2 * 1024 * 1024),
    )(layer_output, tokens_grad)


def solution(mesh):
    in_specs = (
        P(("ctx", "tp"), None),
        P(("ctx", "tp"), None),
        P(None, "tp"),
        P(None, "tp"),
        P(None, "tp"),
        P("tp", None),
        P(),
        P(),
    )
    out_specs = (P(("ctx", "tp"), None), P(("ctx", "tp"), None))
    return jax.shard_map(
        on_device, mesh=mesh, in_specs=in_specs, out_specs=out_specs, check_vma=False
    )
```
